512 devices in a mesh: dp: 4 (over y), expert: 32 (over z, core), tensor: 4 (over x).
Axes of the slice: x: 4, y: 4, z: 16, core: 2. Of those that a mesh axis runs over, the one named last changes fastest.
Arguments:
- tokens: bfloat16 [16384, 2048], P(('dp', 'expert')), may hold values from -6 to 6
- cotangent: bfloat16 [16384, 2048], P(('dp', 'expert')), may hold values from -6 to 6
- expert_ids: int32 [16384, 1], P(('dp', 'expert')), may hold values from 0 to 31; in each aligned block of 128 rows (0 to 127, 128 to 255, ...) at most 8 rows name the same one
- gate_weight: bfloat16 [32, 2048, 1408], P('expert', 'dp', 'tensor'), may hold values from -0.125 to 0.125
- up_weight: bfloat16 [32, 2048, 1408], P('expert', 'dp', 'tensor'), may hold values from -0.125 to 0.125
- down_weight: bfloat16 [32, 2048, 1408], P('expert', 'dp', 'tensor'), may hold values from -0.15625 to 0.15625
Outputs:
- grad_tokens: bfloat16 [16384, 2048], P(('dp', 'expert'), 'tensor')
- grad_gate: bfloat16 [32, 2048, 1408], P('expert', 'dp', 'tensor')
- grad_up: bfloat16 [32, 2048, 1408], P('expert', 'dp', 'tensor')
The draws below stay inside these ranges and needn't reach their ends.
Inputs may be any that keep to these rules, and one draw needn't show every extreme that they name: `expert_ids`: among the 128 tokens of one block no expert id occurs more than 8 times, and in every draw some block holds some id exactly 8 times.
All inputs are finite; a program needn't handle non-finite values.
Results may differ from the reference program's by a relative error of at most 0.013.
Values may be sent and summed in bfloat16 or wider, within the bound.
A program may use at most 64 MiB of HBM per device.

```python
import math
import jax
import jax.numpy as jnp
import numpy as np
from jax import lax

D = 2048
FF = 1408
EXPERTS = 32
TOK_DEV = 128
CAP = 8
TOKENS = 16384
N_DP = 4
N_EXPERT = 32
N_TENSOR = 4


def steps_of(key, extent, split, smallest, top_value):
    loudness, own = 1.0, jax.random.fold_in(key, 6)
    for axis_at, blocks in split:
        heights = jnp.exp(jax.random.uniform(jax.random.fold_in(own, axis_at), (blocks,), jnp.float32, smallest / len(split), top_value / len(split)))
        loudness = loudness * jnp.repeat(heights, extent[axis_at] // blocks).reshape([-1 if axis == axis_at else 1 for axis in range(len(extent))])
    return loudness


def assign_block(key, own, number, rows, count, top, most, skew):
    order = jax.random.permutation(key, count)
    heavy_load, usual = portions_of(count, rows * top, most, skew, True), portions_of(count, rows * top, most, skew, False)
    places = jnp.arange(count)

    def named(sizes, rotation):
        used = int((sizes > 0).sum())
        fixed = max(1, used // 4)
        passed = fixed + (places - fixed + rotation * (used - fixed)) % max(1, count - fixed)
        return jnp.zeros((count,), jnp.int32).at[order[jnp.where(places < fixed, places, passed)]].set(jnp.asarray(sizes, jnp.int32))

    sizes = jnp.where(number % 4 == 0, named(heavy_load, number // 4), named(usual, number - number // 4 - 1))
    mixed = jax.random.permutation(jax.random.fold_in(own, 3), count)
    source_of, receiver = mixed[0:count // 2 * 2:2], mixed[1:count // 2 * 2:2]
    margin = jnp.minimum(sizes[source_of] - 1, most - sizes[receiver]) // 2
    margin = jnp.where((source_of == order[0]) | (receiver == order[0]) | (sizes[receiver] == 0), 0, jnp.maximum(margin, 0))
    passed = jax.random.randint(jax.random.fold_in(own, 4), (count // 2,), 0, 1 << 20) % (margin + 1)
    sizes = sizes.at[source_of].add(-passed).at[receiver].add(passed)
    members = jnp.searchsorted(jnp.cumsum(sizes), jnp.arange(rows * top), side="right").astype(jnp.int32)
    grid = members.reshape(top, rows).T
    grid = grid[jax.random.permutation(jax.random.fold_in(own, 1), rows)]
    rotation = jax.random.randint(jax.random.fold_in(own, 2), (rows, 1), 0, top)
    return jnp.take_along_axis(grid, (jnp.arange(top)[None, :] + rotation) % top, axis=1)


def portions_of(amount, total, bound, slope, full):
    weights = [(1 << 20) // math.isqrt(standing ** slope) + 1 for standing in range(1, amount + 1)]
    largest = bound if full else min(bound, max(-(-total // amount), total * weights[0] // sum(weights)))
    least = 1 if total - largest >= amount - 1 else 0
    counts, rest = [largest] + [least] * (amount - 1), total - largest - least * (amount - 1)
    while rest > 0:
        movable = [i for i in range(1, amount) if counts[i] < largest] or [i for i in range(1, amount) if counts[i] < bound]
        whole, budget = sum([weights[i] for i in movable]), rest
        for i in movable:
            addition = min(bound - counts[i], max(1, budget * weights[i] // whole), rest)
            counts[i] = counts[i] + addition
            rest = rest - addition
    return np.array(counts)


def centred(own_key, dims, scale, bound, cuts=(), kind=jnp.bfloat16):
    gain = steps_of(own_key, dims, cuts, -0.22, 0.18) if cuts else 1.0
    drawn = jax.random.normal(own_key, dims, jnp.float32) * scale * gain
    return jnp.minimum(jnp.maximum(drawn, -bound), bound).astype(kind)


def setup_inputs(seed: int = 0) -> dict:
    key_of = jax.random.split(jax.random.key(seed), 7)
    tokens = centred(key_of[0], (TOKENS, D), 1.0, 6.0, ((0, 128),))
    cotangent = centred(key_of[1], (TOKENS, D), 1.0, 6.0, ((0, 128),))
    expert_ids_keys = jax.random.split(jax.random.fold_in(key_of[2], 1), TOKENS // TOK_DEV)
    expert_ids_turns = jax.random.permutation(jax.random.fold_in(key_of[2], 3), TOKENS // TOK_DEV)
    expert_ids = jax.vmap(lambda own, number: assign_block(jax.random.fold_in(key_of[2], 2), own, number, TOK_DEV, EXPERTS, 1, CAP, 2))(expert_ids_keys, expert_ids_turns).reshape((TOKENS, 1))
    gate_weight = centred(key_of[3], (EXPERTS, D, FF), D ** -0.5, 0.125, ((0, 32), (1, 4), (2, 4)))
    up_weight = centred(key_of[4], (EXPERTS, D, FF), D ** -0.5, 0.125, ((0, 32), (1, 4), (2, 4)))
    down_weight = centred(key_of[5], (EXPERTS, D, FF), FF ** -0.5, 0.15625, ((0, 32), (1, 4), (2, 4)))
    return {"tokens": tokens, "cotangent": cotangent, "expert_ids": expert_ids, "gate_weight": gate_weight, "up_weight": up_weight, "down_weight": down_weight}


def reference(tokens, cotangent, expert_ids, gate_weight, up_weight, down_weight):
    block_count = N_DP * N_EXPERT
    chosen = expert_ids[:, 0].reshape(block_count, TOK_DEV)
    columns = jnp.arange(EXPERTS, dtype=jnp.int32)
    onehot = (chosen[:, :, None] == columns[None, None, :]).astype(jnp.int32)
    earlier = jnp.cumsum(onehot, axis=1) - onehot
    position = jnp.sum(earlier * onehot, axis=2).astype(jnp.int32)
    block_index = jnp.arange(block_count, dtype=jnp.int32)[:, None]
    group_index = block_index // N_EXPERT
    source = block_index % N_EXPERT
    flat_rows = ((chosen * N_DP + group_index) * N_EXPERT + source) * CAP + position
    slot_table = jnp.full((EXPERTS * N_DP * N_EXPERT * CAP,), TOKENS, jnp.int32)
    slot_table = slot_table.at[flat_rows.reshape(-1).astype(jnp.int32)].set(jnp.arange(TOKENS, dtype=jnp.int32))
    slot_index = slot_table.reshape(EXPERTS, N_DP * N_EXPERT * CAP)
    zero_row = jnp.zeros((1, D), jnp.bfloat16)
    tokens_padded = jnp.concatenate([tokens, zero_row.astype(tokens.dtype)], 0)
    cotangent_padded = jnp.concatenate([cotangent, zero_row.astype(cotangent.dtype)], 0)
    shard_width = FF // N_TENSOR
    group_rows = N_EXPERT * CAP

    def one_expert(operands):
        row_index, gate_mat, up_mat, down_mat = operands
        slot_tokens = tokens_padded[row_index]
        slot_cotangent = cotangent_padded[row_index]
        gate_act = jnp.dot(slot_tokens, gate_mat, preferred_element_type=jnp.float32)
        up_act = jnp.dot(slot_tokens, up_mat, preferred_element_type=jnp.float32)
        hidden_grad = jnp.dot(slot_cotangent, down_mat, preferred_element_type=jnp.float32)
        sigmoid_gate = jax.nn.sigmoid(gate_act)
        up_grad = (hidden_grad * gate_act * sigmoid_gate).astype(jnp.bfloat16)
        gate_grad = (hidden_grad * up_act * sigmoid_gate * (1.0 + gate_act * (1.0 - sigmoid_gate))).astype(jnp.bfloat16)
        summed = jnp.zeros((slot_tokens.shape[0], D), jnp.float32)
        for shard in range(N_TENSOR):
            start = shard * shard_width
            shard_term = jnp.dot(gate_grad[:, start:start + shard_width], gate_mat[:, start:start + shard_width].T, preferred_element_type=jnp.float32)
            shard_term = shard_term + jnp.dot(up_grad[:, start:start + shard_width], up_mat[:, start:start + shard_width].T, preferred_element_type=jnp.float32)
            rounded = lax.optimization_barrier(shard_term.astype(jnp.bfloat16))
            summed = summed + rounded.astype(jnp.float32)
        token_rows = summed.astype(jnp.bfloat16)
        grouped_tokens = slot_tokens.reshape(N_DP, group_rows, D).astype(jnp.float32)
        grouped_gate = gate_grad.reshape(N_DP, group_rows, FF).astype(jnp.float32)
        grouped_up = up_grad.reshape(N_DP, group_rows, FF).astype(jnp.float32)
        gate_terms = jnp.einsum("gsd,gsf->gdf", grouped_tokens, grouped_gate)
        up_terms = jnp.einsum("gsd,gsf->gdf", grouped_tokens, grouped_up)
        gate_terms = lax.optimization_barrier(gate_terms.astype(jnp.bfloat16))
        up_terms = lax.optimization_barrier(up_terms.astype(jnp.bfloat16))
        gate_total = jnp.sum(gate_terms.astype(jnp.float32), axis=0).astype(jnp.bfloat16)
        up_total = jnp.sum(up_terms.astype(jnp.float32), axis=0).astype(jnp.bfloat16)
        return token_rows, gate_total, up_total

    token_rows, grad_gate, grad_up = lax.map(one_expert, (slot_index, gate_weight, up_weight, down_weight))
    grad_tokens = jnp.zeros((TOKENS + 1, D), token_rows.dtype)
    grad_tokens = grad_tokens.at[slot_index.reshape(-1)].set(token_rows.reshape(-1, D))
    return grad_tokens[:TOKENS], grad_gate, grad_up
```

```python
import jax
import jax.numpy as jnp
from jax import lax
from jax.sharding import PartitionSpec as P

CAP = 8


def bucket_matrix(expert_ids, expert_count, capacity):
    chosen = expert_ids[:, 0]
    columns = jnp.arange(expert_count, dtype=jnp.int32)
    onehot = (chosen[:, None] == columns[None, :]).astype(jnp.int32)
    earlier = jnp.cumsum(onehot, axis=0) - onehot
    position = jnp.sum(earlier * onehot, axis=1)
    target = chosen * capacity + position
    slot_rows = jnp.arange(expert_count * capacity, dtype=jnp.int32)
    return (slot_rows[:, None] == target[None, :]).astype(jnp.bfloat16)


def on_device(tokens, cotangent, expert_ids, gate_weight, up_weight, down_weight):
    owners = lax.axis_size("expert")
    shards = lax.axis_size("tensor")
    features = tokens.shape[1]
    part = features // shards
    local_experts = gate_weight.shape[0]
    expert_count = local_experts * owners
    slot_count = owners * CAP
    placer = bucket_matrix(expert_ids, expert_count, CAP)
    gate_full, down_full, up_full = (
        lax.all_gather(w, "dp", axis=1, tiled=True)[0] for w in (gate_weight, down_weight, up_weight)
    )
    start = lax.axis_index("tensor") * part
    mine = jnp.concatenate(
        [lax.dynamic_slice_in_dim(a, start, part, axis=1) for a in (tokens, cotangent)], axis=1
    )
    packed = jnp.dot(placer, mine, preferred_element_type=jnp.float32).astype(jnp.bfloat16)
    arrived = lax.all_to_all(
        packed.reshape(owners, CAP, 2 * part), "expert", split_axis=0, concat_axis=0, tiled=True
    ).reshape(slot_count, 2 * part)
    whole = lax.all_gather(arrived, "tensor", axis=0, tiled=False)
    inputs = jnp.concatenate([whole[t, :, :part] for t in range(shards)], axis=1)
    grads_in = jnp.concatenate([whole[t, :, part:] for t in range(shards)], axis=1)
    gate_act = jnp.dot(inputs, gate_full, preferred_element_type=jnp.float32)
    hidden_grad = jnp.dot(grads_in, down_full, preferred_element_type=jnp.float32)
    up_act = jnp.dot(inputs, up_full, preferred_element_type=jnp.float32)
    sigmoid_gate = jax.nn.sigmoid(gate_act)
    up_grad = (hidden_grad * gate_act * sigmoid_gate).astype(jnp.bfloat16)
    gate_grad = (
        hidden_grad * up_act * sigmoid_gate * (1.0 + gate_act * (1.0 - sigmoid_gate))
    ).astype(jnp.bfloat16)
    contract = (((1,), (1,)), ((), ()))
    partial_value = lax.dot_general(gate_grad, gate_full, contract, preferred_element_type=jnp.float32)
    partial_value = partial_value + lax.dot_general(
        up_grad, up_full, contract, preferred_element_type=jnp.float32
    )
    rows = (((0,), (0,)), ((), ()))
    gate_term = lax.dot_general(inputs, gate_grad, rows, preferred_element_type=jnp.float32)
    up_term = lax.dot_general(inputs, up_grad, rows, preferred_element_type=jnp.float32)
    summed = lax.psum_scatter(
        partial_value.astype(jnp.bfloat16), "tensor", scatter_dimension=1, tiled=True
    )
    grad_gate, grad_up = (
        lax.psum_scatter(term.astype(jnp.bfloat16), "dp", scatter_dimension=0, tiled=True)[None]
        for term in (gate_term, up_term)
    )
    returned = lax.all_to_all(
        summed.reshape(owners, CAP, part), "expert", split_axis=0, concat_axis=0, tiled=True
    ).reshape(slot_count, part)
    per_token = lax.dot_general(placer, returned, rows, preferred_element_type=jnp.float32)
    return (per_token.astype(jnp.bfloat16), grad_gate, grad_up)


def solution(mesh):
    placed = (
        P(("dp", "expert"), None),
        P(("dp", "expert"), None),
        P(("dp", "expert"), None),
        P("expert", "dp", "tensor"),
        P("expert", "dp", "tensor"),
        P("expert", "dp", "tensor"),
    )
    return jax.shard_map(
        on_device,
        mesh=mesh,
        in_specs=placed,
        out_specs=(
            P(("dp", "expert"), "tensor"),
            P("expert", "dp", "tensor"),
            P("expert", "dp", "tensor"),
        ),
        check_vma=False,
    )
```

```python
import functools

import jax
import jax.numpy as jnp
from jax import lax
from jax.experimental import pallas as pl
from jax.experimental.pallas import tpu as pltpu
from jax.sharding import PartitionSpec as P

CAP = 8
CORES = 2
LAG = 4
F32 = jnp.float32
BF16 = jnp.bfloat16
MESH = pl.DeviceIdType.MESH


def nt(a, b):
    return lax.dot_general(a, b, (((1,), (1,)), ((), ())), preferred_element_type=F32)


def nn(a, b):
    return lax.dot_general(a, b, (((1,), (0,)), ((), ())), preferred_element_type=F32)


def tn(a, b):
    return lax.dot_general(a, b, (((0,), (0,)), ((), ())), preferred_element_type=F32)


def kernel(
    sizes,
    ids_hbm, tokens_hbm, cotangent_hbm, gate_hbm, up_hbm, down_hbm,
    out_rows, out_gate, out_up,
    ids, mine, sbuf, afull, wfull, placer, acc, gact, tfull, wsum, pbuf, x1, x2, rbuf, back,
    ins, zs, zr, xg_s, xg_r, xh_s, xh_r, ws, wr, vs, vr, bs, br, p1_s, p1_r, p2_s, p2_r,
    as_s, as_r, ah_s, ah_r, e_s, e_r, f1_s, f1_r, f2_s, f2_r, known,
):
    n_dp, n_expert, n_tensor = sizes
    i, e, t = lax.axis_index("dp"), lax.axis_index("expert"), lax.axis_index("tensor")
    z, core = lax.div(e, CORES), lax.rem(e, CORES)
    chips = n_expert // CORES
    half_ring = chips // 2
    block, features = tokens_hbm.shape
    part = features // n_tensor
    width = part // n_dp
    rows = n_expert * CAP
    hidden = gate_hbm.shape[0]
    half_hidden = hidden // 2
    weights = (down_hbm, gate_hbm, up_hbm)
    i_left, i_opp, i_right = (lax.rem(i + k, n_dp) for k in (n_dp - 1, 2, 1))
    t_left, t_opp, t_right = (lax.rem(t + k, n_tensor) for k in (n_tensor - 1, 2, 1))
    y_peer = ({"dp": i_left}, {"dp": i_right})
    x_peer = ({"tensor": t_left}, {"tensor": t_right})
    TO_LEFT, TO_RIGHT = 0, 1

    def copy(src, dst, send, recv, peer):
        return pltpu.make_async_remote_copy(
            src_ref=src, dst_ref=dst, send_sem=send, recv_sem=recv, device_id=peer, device_id_type=MESH
        )

    barrier = pltpu.get_barrier_semaphore()
    other = z * CORES + 1 - core
    z_next, z_prev = lax.rem(z + 1, chips), lax.rem(z + chips - 1, chips)
    near = y_peer + x_peer + ({"dp": i_opp}, {"expert": other})
    near += tuple({"expert": chip * CORES + c} for chip in (z_prev, z_next) for c in range(CORES))
    z_peer = ({"expert": z_prev * CORES + core}, {"expert": z_next * CORES + core})
    for peer in near:
        pl.semaphore_signal(barrier, inc=1, device_id=peer, device_id_type=MESH)

    fetch_rows = [pltpu.make_async_copy(ids_hbm, ids, ins.at[0])]
    for kind, array in enumerate((tokens_hbm, cotangent_hbm)):
        for j in range(n_dp):
            columns = pl.ds(pl.multiple_of(j * part + t * width, width), width)
            fetch_rows.append(
                pltpu.make_async_copy(
                    array.at[:, columns], mine.at[kind, :, pl.ds(j * width, width)], ins.at[1 + kind * n_dp + j]
                )
            )
    fetch_weights = [pltpu.make_async_copy(weights[k], wfull.at[k, 3], ins.at[1 + 2 * n_dp + k]) for k in range(3)]
    for fetch in fetch_rows + fetch_weights:
        fetch.start()

    def weight_first(k, d):
        return copy(weights[k], wfull.at[k, 2 if d == TO_LEFT else 0], ws.at[k, d], wr.at[k, d], y_peer[d])

    def weight_second(k, d):
        cut = pl.ds(0 if d == TO_RIGHT else half_hidden, half_hidden)
        return copy(
            wfull.at[k, 0 if d == TO_RIGHT else 2, cut], wfull.at[k, 1, cut], vs.at[k, d], vr.at[k, d], y_peer[d]
        )

    def weight_forward(k):
        for d in range(2):
            weight_first(k, d).wait_recv()
            weight_second(k, d).start()

    pl.semaphore_wait(barrier, len(near))
    for k in range(3):
        for d in range(2):
            weight_first(k, d).start()

    def report(d):
        pl.semaphore_signal(known.at[d], inc=1, device_id=z_peer[d], device_id_type=MESH)

    report(0)
    report(1)

    for fetch in fetch_rows:
        fetch.wait()
    chosen = ids[...]
    onehot = (lax.broadcasted_iota(jnp.int32, (n_expert, block), 0) == chosen).astype(BF16)
    before = (
        lax.broadcasted_iota(jnp.int32, (block, block), 0) < lax.broadcasted_iota(jnp.int32, (block, block), 1)
    ).astype(BF16)
    earlier = nn(onehot, before)
    position = jnp.sum(earlier * onehot.astype(F32), axis=0, keepdims=True).astype(jnp.int32)
    target = chosen * CAP + position
    placer[...] = (lax.broadcasted_iota(jnp.int32, (rows, block), 0) == target).astype(BF16)
    for kind in range(2):
        sbuf[:, pl.ds(kind * part, part)] = nn(placer[...], mine[kind]).astype(BF16)

    def eight(k):
        return pl.ds(pl.multiple_of(k * CAP, CAP), CAP)

    def both(k):
        return pl.ds(pl.multiple_of(k * (CORES * CAP), CORES * CAP), CORES * CAP)

    def expert_at(away, c):
        return lax.rem(z + away, chips) * CORES + c

    def back_from(away):
        return lax.rem(chips - away, chips)

    def dispatch(away, c):
        to, place = expert_at(away, c), back_from(away) * CORES + core
        return copy(
            sbuf.at[eight(to)], afull.at[t, eight(place)], zs.at[away * CORES + c], zr.at[place], {"expert": to}
        )

    def arrived(away, c):
        place = away * CORES + c
        copy(
            sbuf.at[eight(other)], afull.at[t, eight(place)], zs.at[place], zr.at[place], {"expert": other}
        ).wait_recv()

    def send_to(away):
        for c in range(CORES):
            dispatch(away, c).start()

    dispatch(0, 1 - core).start()
    own = pltpu.make_async_copy(sbuf.at[eight(e)], afull.at[t, eight(core)], zs.at[core])
    own.start()
    send_to(1)
    send_to(chips - 1)

    def send_further(m, carry):
        for d in range(2):
            pl.semaphore_wait(known.at[d], 1)
            report(d)
        send_to(m + 1)
        send_to(chips - m - 1)
        return carry

    lax.fori_loop(1, half_ring - 1, send_further, 0)
    for d in range(2):
        pl.semaphore_wait(known.at[d], 1)
    send_to(half_ring)

    def chunk(m):
        odd = lax.rem(m, 2)
        return lax.rem(odd * (chips - lax.div(m + 1, 2)) + (1 - odd) * lax.div(m, 2), chips)

    def spread_first(q, m, d):
        c = both(chunk(m))
        return copy(afull.at[q, c], afull.at[q, c], xg_s.at[d, m], xg_r.at[d, m], x_peer[d])

    def spread_second(q, m, d):
        c = eight(chunk(m) * CORES + (0 if d == TO_RIGHT else 1))
        return copy(afull.at[q, c], afull.at[q, c], xh_s.at[d, m], xh_r.at[d, m], x_peer[d])

    def spread_own(m):
        for d in range(2):
            spread_first(t, m, d).start()

    def forward(m):
        for d in range(2):
            from_q = t_left if d == TO_RIGHT else t_right
            spread_first(from_q, m, d).wait_recv()
            spread_second(from_q, m, d).start()

    def take(m, carry):
        for c in range(CORES):
            arrived(chunk(m), c)
        spread_own(m)
        return carry

    def take_and_forward(m, carry):
        take(m, carry)
        forward(m - LAG)
        return carry

    def forward_only(m, carry):
        forward(m)
        return carry

    own.wait()
    arrived(0, 1 - core)
    spread_own(0)
    lax.fori_loop(1, LAG, take, 0)
    lax.fori_loop(LAG, 11, take_and_forward, 0)
    weight_forward(0)
    lax.fori_loop(11, 15, take_and_forward, 0)
    weight_forward(1)
    lax.fori_loop(15, chips, take_and_forward, 0)
    lax.fori_loop(chips - LAG, chips, forward_only, 0)
    weight_forward(2)

    def exchange(r):
        j = lax.rem(i + r, n_dp)
        columns = pl.ds(pl.multiple_of(j * width, width), width)
        return copy(afull.at[t, :, columns], tfull.at[t, r - 1], e_s.at[r - 1], e_r.at[r - 1], {"dp": j})

    for r in range(1, n_dp):
        exchange(r).start()

    def finish_rows(m, carry):
        for d in range(2):
            spread_second(t_opp, m, d).wait_recv()
        return carry

    lax.fori_loop(0, chips, finish_rows, 0)
    for fetch in fetch_weights:
        fetch.wait()

    def rows_of(j, kind):
        columns = pl.ds(pl.multiple_of(kind * part + j * width, width), width)
        return jnp.concatenate([afull[q, :, columns] for q in range(n_tensor)], axis=1)

    for k, kind in enumerate((1, 0, 0)):
        acc[k] = nt(wfull[k, 3], rows_of(i, kind))
        acc[k] += nt(wfull[k, 0], rows_of(i_left, kind))
        acc[k] += nt(wfull[k, 2], rows_of(i_right, kind))
        for d in range(2):
            weight_second(k, d).wait_recv()
        acc[k] += nt(wfull[k, 1], rows_of(i_opp, kind))

    hidden_grad, gate_act, up_act = acc[0], acc[1], acc[2]
    sigmoid_gate = jax.nn.sigmoid(gate_act)
    scaled = hidden_grad * sigmoid_gate
    gact[3, 0] = (scaled * up_act * (1.0 + gate_act * (1.0 - sigmoid_gate))).astype(BF16)
    gact[3, 1] = (scaled * gate_act).astype(BF16)

    def act_first(d):
        return copy(gact.at[3], gact.at[2 if d == TO_LEFT else 0], as_s.at[d], as_r.at[d], y_peer[d])

    def act_second(d):
        k = 0 if d == TO_RIGHT else 1
        return copy(gact.at[0 if d == TO_RIGHT else 2, k], gact.at[1, k], ah_s.at[d], ah_r.at[d], y_peer[d])

    for d in range(2):
        act_first(d).start()

    def input_term(r):
        q = lax.rem(t + r, n_tensor)
        slot = 3 - lax.rem(q + n_dp - i, n_dp)
        pbuf[r] = (tn(gact[3, 0], wfull[1, slot]) + tn(gact[3, 1], wfull[2, slot])).astype(BF16)

    piece = rows // 4
    cuts = ((pl.ds(piece, piece), pl.ds(2 * piece, piece)), (pl.ds(0, piece), pl.ds(3 * piece, piece)))

    def part_hop(d, far):
        cut = cuts[far][0 if d == TO_RIGHT else 1]
        return copy(pbuf.at[2, cut], x1.at[d, far], p1_s.at[d, far], p1_r.at[d, far], x_peer[d])

    def part_last(d, far, h):
        cut = cuts[far][h]
        r = 1 if d == TO_RIGHT else 3
        return copy(pbuf.at[r, cut], x2.at[d, cut], p2_s.at[d, far, h], p2_r.at[d, far, h], x_peer[d])

    def relay(far):
        for d, r, h in ((TO_RIGHT, 1, 0), (TO_LEFT, 3, 1)):
            cut = cuts[far][h]
            part_hop(d, far).wait_recv()
            pbuf[r, cut] = (pbuf[r, cut].astype(F32) + x1[d, far].astype(F32)).astype(BF16)
            part_last(d, far, h).start()

    def own_half(far):
        part_last(TO_RIGHT, far, 1).start()
        part_last(TO_LEFT, far, 0).start()

    input_term(2)
    for far in range(2):
        for d in range(2):
            part_hop(d, far).start()
    input_term(1)
    input_term(3)
    own_half(0)
    relay(0)
    own_half(1)
    relay(1)
    input_term(0)

    def share_first(d):
        return copy(tfull.at[t], tfull.at[t], f1_s.at[d], f1_r.at[d], x_peer[d])

    def share_second(q, d):
        cut = pl.ds(0 if d == TO_RIGHT else rows // 2, rows // 2)
        return copy(tfull.at[q, :, cut], tfull.at[q, :, cut], f2_s.at[d], f2_r.at[d], x_peer[d])

    for r in range(1, n_dp):
        exchange(r).wait_recv()
    for d in range(2):
        share_first(d).start()

    def give_back(away, c):
        place = away * CORES + c
        to = expert_at(away, c)
        return copy(
            rbuf.at[eight(place)], back.at[eight(e)], bs.at[place], br.at[back_from(away) * CORES + core], {"expert": to}
        )

    def add_up(far):
        for h in range(2):
            cut = cuts[far][h]
            for d in range(2):
                part_last(d, far, h).wait_recv()
            total = pbuf[0, cut].astype(F32) + x2[0, cut].astype(F32) + x2[1, cut].astype(F32)
            rbuf[cut, :] = total.astype(BF16)

    def give(m, carry):
        for c in range(CORES):
            give_back(half_ring + m, c).start()
            give_back(half_ring - 1 - m, c).start()
        return carry

    quarter_ring = half_ring // 2
    add_up(0)
    lax.fori_loop(0, quarter_ring, give, 0)
    for d in range(2):
        act_first(d).wait_recv()
        act_second(d).start()
    add_up(1)
    lax.fori_loop(quarter_ring, half_ring - 1, give, 0)
    for c in range(CORES):
        give_back(chips - 1, c).start()
    give_back(0, 1 - core).start()
    kept = pltpu.make_async_copy(rbuf.at[eight(core)], back.at[eight(e)], bs.at[core])
    kept.start()
    for d in range(2):
        share_first(d).wait_recv()
        share_second(t_left if d == TO_RIGHT else t_right, d).start()

    for k in range(2):
        wsum[k] = nn(gact[3, k], rows_of(i, 0))
    for d in range(2):
        share_second(t_opp, d).wait_recv()

    def group_rows(r):
        return jnp.concatenate([tfull[q, r - 1] for q in range(n_tensor)], axis=1)

    for k in range(2):
        wsum[k] += nn(gact[0, k], group_rows(1)) + nn(gact[2, k], group_rows(3))
    for d in range(2):
        act_second(d).wait_recv()
    for k, out in enumerate((out_gate, out_up)):
        out[...] = (wsum[k] + nn(gact[1, k], group_rows(2))).astype(BF16)

    def returned(away, c):
        place = away * CORES + c
        source = expert_at(away, c)
        copy(rbuf.at[eight(place)], back.at[eight(source)], bs.at[place], br.at[place], {"expert": other}).wait_recv()

    def take_back(away, carry):
        for c in range(CORES):
            returned(away, c)
        return carry

    kept.wait()
    returned(0, 1 - core)
    lax.fori_loop(1, chips, take_back, 0)
    out_rows[...] = tn(placer[...], back[...]).astype(BF16)

    dispatch(0, 1 - core).wait_send()
    give_back(0, 1 - core).wait_send()

    def sent(away, carry):
        for c in range(CORES):
            dispatch(away, c).wait_send()
            give_back(away, c).wait_send()
        return carry

    lax.fori_loop(1, chips, sent, 0)

    def spread_sent(m, carry):
        for d in range(2):
            spread_first(t, m, d).wait_send()
            spread_second(t_left if d == TO_RIGHT else t_right, m, d).wait_send()
        return carry

    lax.fori_loop(0, chips, spread_sent, 0)
    for r in range(1, n_dp):
        exchange(r).wait_send()
    for d in range(2):
        act_first(d).wait_send()
        act_second(d).wait_send()
        share_first(d).wait_send()
        share_second(t_left if d == TO_RIGHT else t_right, d).wait_send()
        for far in range(2):
            part_hop(d, far).wait_send()
            for h in range(2):
                part_last(d, far, h).wait_send()
        for k in range(3):
            weight_first(k, d).wait_send()
            weight_second(k, d).wait_send()


def on_device(sizes, tokens, cotangent, expert_ids, gate_weight, up_weight, down_weight):
    n_dp, n_expert, n_tensor = sizes
    block, features = tokens.shape
    hidden, depth = gate_weight.shape[2], gate_weight.shape[1]
    part, rows, chips = features // n_tensor, n_expert * CAP, n_expert // CORES
    dma = pltpu.SemaphoreType.DMA
    flip = lambda w: jnp.swapaxes(w, 1, 2)[0]
    operands = (expert_ids.reshape(1, block), tokens, cotangent, flip(gate_weight), flip(up_weight), flip(down_weight))
    grad_rows, grad_gate, grad_up = pl.pallas_call(
        functools.partial(kernel, sizes),
        out_shape=(
            jax.ShapeDtypeStruct((block, part), BF16),
            jax.ShapeDtypeStruct((hidden, depth), BF16),
            jax.ShapeDtypeStruct((hidden, depth), BF16),
        ),
        in_specs=[pl.BlockSpec(memory_space=pltpu.HBM)] * 6,
        out_specs=[pl.BlockSpec(memory_space=pltpu.VMEM)] * 3,
        scratch_shapes=[
            pltpu.VMEM((1, block), jnp.int32),
            pltpu.VMEM((2, block, part), BF16),
            pltpu.VMEM((rows, 2 * part), BF16),
            pltpu.VMEM((n_tensor, rows, 2 * part), BF16),
            pltpu.VMEM((3, n_dp, hidden, depth), BF16),
            pltpu.VMEM((rows, block), BF16),
            pltpu.VMEM((3, hidden, rows), F32),
            pltpu.VMEM((n_dp, 2, hidden, rows), BF16),
            pltpu.VMEM((n_tensor, n_dp - 1, rows, part // n_dp), BF16),
            pltpu.VMEM((2, hidden, depth), F32),
            pltpu.VMEM((n_tensor, rows, part), BF16),
            pltpu.VMEM((2, 2, rows // 4, part), BF16),
            pltpu.VMEM((2, rows, part), BF16),
            pltpu.VMEM((rows, part), BF16),
            pltpu.VMEM((rows, part), BF16),
            dma((1 + 2 * n_dp + 3,)), dma((n_expert,)), dma((n_expert,)),
            dma((2, chips)), dma((2, chips)), dma((2, chips)), dma((2, chips)),
            dma((3, 2)), dma((3, 2)), dma((3, 2)), dma((3, 2)),
            dma((n_expert,)), dma((n_expert,)),
            dma((2, 2)), dma((2, 2)), dma((2, 2, 2)), dma((2, 2, 2)),
            dma((2,)), dma((2,)), dma((2,)), dma((2,)),
            dma((n_dp - 1,)), dma((n_dp - 1,)),
            dma((2,)), dma((2,)), dma((2,)), dma((2,)),
            pltpu.SemaphoreType.REGULAR((2,)),
        ],
        compiler_params=pltpu.CompilerParams(
            collective_id=0, has_side_effects=True, vmem_limit_bytes=48 << 20
        ),
        name="moe_backward",
    )(*(pltpu.with_memory_space_constraint(a, pltpu.HBM) for a in operands))
    back = lambda g: jnp.swapaxes(g[None], 1, 2)
    return grad_rows, back(grad_gate), back(grad_up)


def solution(mesh):
    sizes = tuple(mesh.shape[a] for a in ("dp", "expert", "tensor"))
    row, weight = P(("dp", "expert"), None), P("expert", "dp", "tensor")
    return jax.shard_map(
        functools.partial(on_device, sizes),
        mesh=mesh,
        in_specs=(row, row, row, weight, weight, weight),
        out_specs=(P(("dp", "expert"), "tensor"), weight, weight),
        check_vma=False,
    )
```

```python
import functools

import jax
import jax.numpy as jnp
from jax import lax
from jax.experimental import pallas as pl
from jax.experimental.pallas import tpu as pltpu
from jax.sharding import PartitionSpec as P

CAP = 8
CORES = 2
LAG = 4
EARLY = 4
PIECES = 4
F32 = jnp.float32
BF16 = jnp.bfloat16
MESH = pl.DeviceIdType.MESH


def nt(a, b):
    return lax.dot_general(a, b, (((1,), (1,)), ((), ())), preferred_element_type=F32)


def nn(a, b):
    return lax.dot_general(a, b, (((1,), (0,)), ((), ())), preferred_element_type=F32)


def tn(a, b):
    return lax.dot_general(a, b, (((0,), (0,)), ((), ())), preferred_element_type=F32)


def kernel(
    sizes,
    ids_hbm, tokens_hbm, cotangent_hbm, gate_hbm, up_hbm, down_hbm,
    out_rows, out_gate, out_up,
    ids, mine, sbuf, afull, wfull, placer, acc, gact, tfull, wsum, pbuf, x1, x2, rbuf, back,
    ins, zs, zr, xg_s, xg_r, xh_s, xh_r, ws, wr, vs, vr, bs, br, p1_s, p1_r, p2_s, p2_r,
    as_s, as_r, ah_s, ah_r, e_s, e_r, f1_s, f1_r, f2_s, f2_r, known,
):
    n_dp, n_expert, n_tensor = sizes
    i, e, t = lax.axis_index("dp"), lax.axis_index("expert"), lax.axis_index("tensor")
    z, core = lax.div(e, CORES), lax.rem(e, CORES)
    chips = n_expert // CORES
    half_ring = chips // 2
    block, features = tokens_hbm.shape
    part = features // n_tensor
    width = part // n_dp
    rows = n_expert * CAP
    hidden = gate_hbm.shape[0]
    half_hidden = hidden // 2
    weights = (gate_hbm, up_hbm, down_hbm)
    i_left, i_opp, i_right = (lax.rem(i + k, n_dp) for k in (n_dp - 1, 2, 1))
    t_left, t_opp, t_right = (lax.rem(t + k, n_tensor) for k in (n_tensor - 1, 2, 1))
    y_peer = ({"dp": i_left}, {"dp": i_right})
    x_peer = ({"tensor": t_left}, {"tensor": t_right})
    TO_LEFT, TO_RIGHT = 0, 1

    def copy(src, dst, send, recv, peer):
        return pltpu.make_async_remote_copy(
            src_ref=src, dst_ref=dst, send_sem=send, recv_sem=recv, device_id=peer, device_id_type=MESH
        )

    barrier = pltpu.get_barrier_semaphore()
    other = z * CORES + 1 - core
    z_next, z_prev = lax.rem(z + 1, chips), lax.rem(z + chips - 1, chips)
    near = y_peer + x_peer + ({"dp": i_opp}, {"expert": other})
    near += tuple({"expert": chip * CORES + c} for chip in (z_prev, z_next) for c in range(CORES))
    z_peer = ({"expert": z_prev * CORES + core}, {"expert": z_next * CORES + core})
    for peer in near:
        pl.semaphore_signal(barrier, inc=1, device_id=peer, device_id_type=MESH)

    fetch_rows = [pltpu.make_async_copy(ids_hbm, ids, ins.at[0])]
    for kind, array in enumerate((tokens_hbm, cotangent_hbm)):
        for j in range(n_dp):
            columns = pl.ds(pl.multiple_of(j * part + t * width, width), width)
            fetch_rows.append(
                pltpu.make_async_copy(
                    array.at[:, columns], mine.at[kind, :, pl.ds(j * width, width)], ins.at[1 + kind * n_dp + j]
                )
            )
    fetch_weights = [pltpu.make_async_copy(weights[k], wfull.at[k, 3], ins.at[1 + 2 * n_dp + k]) for k in range(3)]
    for fetch in fetch_rows + fetch_weights:
        fetch.start()

    def weight_first(k, d):
        return copy(weights[k], wfull.at[k, 2 if d == TO_LEFT else 0], ws.at[k, d], wr.at[k, d], y_peer[d])

    def weight_second(k, d):
        cut = pl.ds(0 if d == TO_RIGHT else half_hidden, half_hidden)
        return copy(
            wfull.at[k, 0 if d == TO_RIGHT else 2, cut], wfull.at[k, 1, cut], vs.at[k, d], vr.at[k, d], y_peer[d]
        )

    def weight_forward(k):
        for d in range(2):
            weight_first(k, d).wait_recv()
            weight_second(k, d).start()

    pl.semaphore_wait(barrier, len(near))
    for k in range(3):
        for d in range(2):
            weight_first(k, d).start()

    def report(d):
        pl.semaphore_signal(known.at[d], inc=1, device_id=z_peer[d], device_id_type=MESH)

    report(0)
    report(1)

    for fetch in fetch_rows:
        fetch.wait()
    chosen = ids[...]
    onehot = (lax.broadcasted_iota(jnp.int32, (n_expert, block), 0) == chosen).astype(BF16)
    before = (
        lax.broadcasted_iota(jnp.int32, (block, block), 0) < lax.broadcasted_iota(jnp.int32, (block, block), 1)
    ).astype(BF16)
    earlier = nn(onehot, before)
    position = jnp.sum(earlier * onehot.astype(F32), axis=0, keepdims=True).astype(jnp.int32)
    target = chosen * CAP + position
    placer[...] = (lax.broadcasted_iota(jnp.int32, (rows, block), 0) == target).astype(BF16)
    for kind in range(2):
        sbuf[:, pl.ds(kind * part, part)] = nn(placer[...], mine[kind]).astype(BF16)

    def eight(k):
        return pl.ds(pl.multiple_of(k * CAP, CAP), CAP)

    def both(k):
        return pl.ds(pl.multiple_of(k * (CORES * CAP), CORES * CAP), CORES * CAP)

    def expert_at(away, c):
        return lax.rem(z + away, chips) * CORES + c

    def dispatch(away, c):
        to = expert_at(away, c)
        return copy(sbuf.at[eight(to)], afull.at[t, eight(e)], zs.at[to], zr.at[e], {"expert": to})

    def arrived(source):
        copy(
            sbuf.at[eight(other)], afull.at[t, eight(source)], zs.at[source], zr.at[source], {"expert": other}
        ).wait_recv()

    def send_to(away):
        for c in range(CORES):
            dispatch(away, c).start()

    dispatch(0, 1 - core).start()
    own = pltpu.make_async_copy(sbuf.at[eight(e)], afull.at[t, eight(e)], zs.at[e])
    own.start()
    send_to(1)
    send_to(chips - 1)

    def send_further(m, carry):
        for d in range(2):
            pl.semaphore_wait(known.at[d], 1)
            report(d)
        send_to(m + 1)
        send_to(chips - m - 1)
        return carry

    lax.fori_loop(1, half_ring - 1, send_further, 0)
    for d in range(2):
        pl.semaphore_wait(known.at[d], 1)
    send_to(half_ring)

    def chunk(m):
        odd = lax.rem(m, 2)
        return lax.rem(z + odd * (chips - lax.div(m + 1, 2)) + (1 - odd) * lax.div(m, 2), chips)

    def spread_first(q, m, d):
        c = both(chunk(m))
        return copy(afull.at[q, c], afull.at[q, c], xg_s.at[d, m], xg_r.at[d, m], x_peer[d])

    def spread_second(q, m, d):
        c = eight(chunk(m) * CORES + (0 if d == TO_RIGHT else 1))
        return copy(afull.at[q, c], afull.at[q, c], xh_s.at[d, m], xh_r.at[d, m], x_peer[d])

    def spread_own(m):
        for d in range(2):
            spread_first(t, m, d).start()

    def forward(m):
        for d in range(2):
            from_q = t_left if d == TO_RIGHT else t_right
            spread_first(from_q, m, d).wait_recv()
            spread_second(from_q, m, d).start()

    def take(m, carry):
        for c in range(CORES):
            arrived(chunk(m) * CORES + c)
        spread_own(m)
        return carry

    def take_and_forward(m, carry):
        take(m, carry)
        forward(m - LAG)
        return carry

    def forward_only(m, carry):
        forward(m)
        return carry

    def exchange(r):
        j = lax.rem(i + r, n_dp)
        columns = pl.ds(pl.multiple_of(j * width, width), width)
        return copy(afull.at[t, :, columns], tfull.at[t, r - 1], e_s.at[r - 1], e_r.at[r - 1], {"dp": j})

    def share_first(d):
        return copy(tfull.at[t], tfull.at[t], f1_s.at[d], f1_r.at[d], x_peer[d])

    def share_second(q, d):
        cut = pl.ds(0 if d == TO_RIGHT else rows // 2, rows // 2)
        return copy(tfull.at[q, :, cut], tfull.at[q, :, cut], f2_s.at[d], f2_r.at[d], x_peer[d])

    def exchange_start():
        for r in range(1, n_dp):
            exchange(r).start()

    def share_start():
        for r in range(1, n_dp):
            exchange(r).wait_recv()
        for d in range(2):
            share_first(d).start()

    def share_forward():
        for d in range(2):
            share_first(d).wait_recv()
            share_second(t_left if d == TO_RIGHT else t_right, d).start()

    early = z < chips // EARLY
    late = z >= chips // EARLY

    own.wait()
    arrived(other)
    spread_own(0)
    lax.fori_loop(1, LAG, take, 0)
    lax.fori_loop(LAG, 11, take_and_forward, 0)
    weight_forward(0)
    lax.fori_loop(11, 15, take_and_forward, 0)
    weight_forward(1)
    lax.fori_loop(15, chips, take_and_forward, 0)
    pl.when(early)(exchange_start)
    lax.fori_loop(chips - LAG, chips, forward_only, 0)
    weight_forward(2)
    pl.when(late)(exchange_start)

    def finish_rows(m, carry):
        for d in range(2):
            spread_second(t_opp, m, d).wait_recv()
        return carry

    lax.fori_loop(0, chips, finish_rows, 0)
    pl.when(early)(share_start)
    for fetch in fetch_weights:
        fetch.wait()

    def rows_of(j, kind):
        columns = pl.ds(pl.multiple_of(kind * part + j * width, width), width)
        return jnp.concatenate([afull[q, :, columns] for q in range(n_tensor)], axis=1)

    def product(k, kind):
        acc[k] = nt(wfull[k, 3], rows_of(i, kind))
        acc[k] += nt(wfull[k, 0], rows_of(i_left, kind))
        acc[k] += nt(wfull[k, 2], rows_of(i_right, kind))

    def product_end(k, kind):
        for d in range(2):
            weight_second(k, d).wait_recv()
        return acc[k] + nt(wfull[k, 1], rows_of(i_opp, kind))

    for k, kind in enumerate((0, 0, 1)):
        product(k, kind)
    gate_act = product_end(0, 0)
    sigmoid_gate = jax.nn.sigmoid(gate_act)
    acc[0] = gate_act * sigmoid_gate
    acc[1] = product_end(1, 0) * (sigmoid_gate * (1.0 + gate_act * (1.0 - sigmoid_gate)))
    hidden_grad = product_end(2, 1)
    gact[3, 0] = (hidden_grad * acc[1]).astype(BF16)
    gact[3, 1] = (hidden_grad * acc[0]).astype(BF16)

    def act_first(k, d):
        return copy(gact.at[3, k], gact.at[2 if d == TO_LEFT else 0, k], as_s.at[k, d], as_r.at[k, d], y_peer[d])

    def act_second(k, d):
        cut = pl.ds(0 if d == TO_RIGHT else half_hidden, half_hidden)
        return copy(
            gact.at[0 if d == TO_RIGHT else 2, k, cut], gact.at[1, k, cut], ah_s.at[k, d], ah_r.at[k, d], y_peer[d]
        )

    def act_forward(k):
        for d in range(2):
            act_first(k, d).wait_recv()
            act_second(k, d).start()

    for k in range(2):
        for d in range(2):
            act_first(k, d).start()

    def input_term(r):
        q = lax.rem(t + r, n_tensor)
        slot = 3 - lax.rem(q + n_dp - i, n_dp)
        pbuf[r] = (tn(gact[3, 0], wfull[0, slot]) + tn(gact[3, 1], wfull[1, slot])).astype(BF16)

    size = rows // 2 // PIECES
    cuts = [[pl.ds(h * rows // 2 + p * size, size) for h in range(2)] for p in range(PIECES)]

    def part_hop(d, p):
        cut = cuts[p][0 if d == TO_RIGHT else 1]
        return copy(pbuf.at[2, cut], x1.at[d, p], p1_s.at[d, p], p1_r.at[d, p], x_peer[d])

    def part_last(d, p, h):
        cut = cuts[p][h]
        r = 1 if d == TO_RIGHT else 3
        return copy(pbuf.at[r, cut], x2.at[d, cut], p2_s.at[d, p, h], p2_r.at[d, p, h], x_peer[d])

    def hop(p):
        for d in range(2):
            part_hop(d, p).start()

    def relay(p):
        for d, r, h in ((TO_RIGHT, 1, 0), (TO_LEFT, 3, 1)):
            cut = cuts[p][h]
            part_hop(d, p).wait_recv()
            pbuf[r, cut] = (pbuf[r, cut].astype(F32) + x1[d, p].astype(F32)).astype(BF16)
            part_last(d, p, h).start()

    def own_half(p):
        part_last(TO_RIGHT, p, 1).start()
        part_last(TO_LEFT, p, 0).start()

    def give_back(to):
        return copy(rbuf.at[eight(to)], back.at[eight(e)], bs.at[to], br.at[e], {"expert": to})

    def add_up(p):
        for h in range(2):
            cut = cuts[p][h]
            for d in range(2):
                part_last(d, p, h).wait_recv()
            total = pbuf[0, cut].astype(F32) + x2[0, cut].astype(F32) + x2[1, cut].astype(F32)
            rbuf[cut, :] = total.astype(BF16)

    def give(place):
        for h in range(2):
            to = h * (n_expert // 2) + place

            @pl.when(to != e)
            def _():
                give_back(to).start()

    def give_piece(p):
        for place in range(p * n_expert // 2 // PIECES, (p + 1) * n_expert // 2 // PIECES):
            give(place)

    input_term(2)
    hop(0)
    hop(1)
    input_term(1)
    input_term(3)
    own_half(0)
    relay(0)
    hop(2)
    own_half(1)
    input_term(0)
    relay(1)
    hop(3)
    pl.when(early)(share_forward)
    own_half(2)
    add_up(0)
    give_piece(0)
    relay(2)
    own_half(3)
    act_forward(0)
    add_up(1)
    give_piece(1)
    relay(3)
    pl.when(late)(share_start)
    add_up(2)
    give_piece(2)
    act_forward(1)
    add_up(3)
    give_piece(3)
    kept = pltpu.make_async_copy(rbuf.at[eight(e)], back.at[eight(e)], bs.at[e])
    kept.start()
    pl.when(late)(share_forward)

    for k in range(2):
        wsum[k] = nn(gact[3, k], rows_of(i, 0))
    for d in range(2):
        share_second(t_opp, d).wait_recv()

    def group_rows(r):
        return jnp.concatenate([tfull[q, r - 1] for q in range(n_tensor)], axis=1)

    for k in range(2):
        wsum[k] += nn(gact[0, k], group_rows(1)) + nn(gact[2, k], group_rows(3))
    for k, out in enumerate((out_gate, out_up)):
        for d in range(2):
            act_second(k, d).wait_recv()
        out[...] = (wsum[k] + nn(gact[1, k], group_rows(2))).astype(BF16)

    def returned(away, c):
        source = expert_at(away, c)
        copy(rbuf.at[eight(other)], back.at[eight(source)], bs.at[other], br.at[source], {"expert": other}).wait_recv()

    def take_back(away, carry):
        for c in range(CORES):
            returned(away, c)
        return carry

    kept.wait()
    returned(0, 1 - core)
    lax.fori_loop(1, chips, take_back, 0)
    out_rows[...] = tn(placer[...], back[...]).astype(BF16)

    dispatch(0, 1 - core).wait_send()
    give_back(other).wait_send()

    def sent(away, carry):
        for c in range(CORES):
            dispatch(away, c).wait_send()
            give_back(expert_at(away, c)).wait_send()
        return carry

    lax.fori_loop(1, chips, sent, 0)

    def spread_sent(m, carry):
        for d in range(2):
            spread_first(t, m, d).wait_send()
            spread_second(t_left if d == TO_RIGHT else t_right, m, d).wait_send()
        return carry

    lax.fori_loop(0, chips, spread_sent, 0)
    for r in range(1, n_dp):
        exchange(r).wait_send()
    for d in range(2):
        for k in range(2):
            act_first(k, d).wait_send()
            act_second(k, d).wait_send()
        share_first(d).wait_send()
        share_second(t_left if d == TO_RIGHT else t_right, d).wait_send()
        for p in range(PIECES):
            part_hop(d, p).wait_send()
            for h in range(2):
                part_last(d, p, h).wait_send()
        for k in range(3):
            weight_first(k, d).wait_send()
            weight_second(k, d).wait_send()


def write_out(*refs):
    count = len(refs) // 2
    copies = [pltpu.make_async_copy(refs[n], refs[count + n], refs[-1].at[n]) for n in range(count)]
    for each in copies:
        each.start()
    for each in copies:
        each.wait()


def on_device(sizes, tokens, cotangent, expert_ids, gate_weight, up_weight, down_weight):
    n_dp, n_expert, n_tensor = sizes
    block, features = tokens.shape
    hidden, depth = gate_weight.shape[2], gate_weight.shape[1]
    part, rows, chips = features // n_tensor, n_expert * CAP, n_expert // CORES
    dma = pltpu.SemaphoreType.DMA
    flip = lambda w: jnp.swapaxes(w, 1, 2)[0]
    operands = (expert_ids.reshape(1, block), tokens, cotangent, flip(gate_weight), flip(up_weight), flip(down_weight))
    grad_rows, grad_gate, grad_up = pl.pallas_call(
        functools.partial(kernel, sizes),
        out_shape=(
            jax.ShapeDtypeStruct((block, part), BF16),
            jax.ShapeDtypeStruct((hidden, depth), BF16),
            jax.ShapeDtypeStruct((hidden, depth), BF16),
        ),
        in_specs=[pl.BlockSpec(memory_space=pltpu.HBM)] * 6,
        out_specs=[pl.BlockSpec(memory_space=pltpu.VMEM)] * 3,
        scratch_shapes=[
            pltpu.VMEM((1, block), jnp.int32),
            pltpu.VMEM((2, block, part), BF16),
            pltpu.VMEM((rows, 2 * part), BF16),
            pltpu.VMEM((n_tensor, rows, 2 * part), BF16),
            pltpu.VMEM((3, n_dp, hidden, depth), BF16),
            pltpu.VMEM((rows, block), BF16),
            pltpu.VMEM((3, hidden, rows), F32),
            pltpu.VMEM((n_dp, 2, hidden, rows), BF16),
            pltpu.VMEM((n_tensor, n_dp - 1, rows, part // n_dp), BF16),
            pltpu.VMEM((2, hidden, depth), F32),
            pltpu.VMEM((n_tensor, rows, part), BF16),
            pltpu.VMEM((2, PIECES, rows // 2 // PIECES, part), BF16),
            pltpu.VMEM((2, rows, part), BF16),
            pltpu.VMEM((rows, part), BF16),
            pltpu.VMEM((rows, part), BF16),
            dma((1 + 2 * n_dp + 3,)), dma((n_expert,)), dma((n_expert,)),
            dma((2, chips)), dma((2, chips)), dma((2, chips)), dma((2, chips)),
            dma((3, 2)), dma((3, 2)), dma((3, 2)), dma((3, 2)),
            dma((n_expert,)), dma((n_expert,)),
            dma((2, PIECES)), dma((2, PIECES)), dma((2, PIECES, 2)), dma((2, PIECES, 2)),
            dma((2, 2)), dma((2, 2)), dma((2, 2)), dma((2, 2)),
            dma((n_dp - 1,)), dma((n_dp - 1,)),
            dma((2,)), dma((2,)), dma((2,)), dma((2,)),
            pltpu.SemaphoreType.REGULAR((2,)),
        ],
        compiler_params=pltpu.CompilerParams(
            collective_id=0, has_side_effects=True, vmem_limit_bytes=48 << 20
        ),
        name="moe_backward",
    )(*(pltpu.with_memory_space_constraint(a, pltpu.HBM) for a in operands))
    results = (grad_rows, grad_gate, grad_up)
    grad_rows, grad_gate, grad_up = pl.pallas_call(
        write_out,
        out_shape=tuple(jax.ShapeDtypeStruct(r.shape, r.dtype) for r in results),
        in_specs=[pl.BlockSpec(memory_space=pltpu.VMEM)] * 3,
        out_specs=[pl.BlockSpec(memory_space=pltpu.HBM)] * 3,
        scratch_shapes=[dma((3,))],
        compiler_params=pltpu.CompilerParams(vmem_limit_bytes=32 << 20),
        name="write_out",
    )(*results)
    back = lambda g: jnp.swapaxes(g[None], 1, 2)
    return grad_rows, back(grad_gate), back(grad_up)


def solution(mesh):
    sizes = tuple(mesh.shape[a] for a in ("dp", "expert", "tensor"))
    row, weight = P(("dp", "expert"), None), P("expert", "dp", "tensor")
    return jax.shard_map(
        functools.partial(on_device, sizes),
        mesh=mesh,
        in_specs=(row, row, row, weight, weight, weight),
        out_specs=(P(("dp", "expert"), "tensor"), weight, weight),
        check_vma=False,
    )
```

```python
import functools

import jax
import jax.numpy as jnp
from jax import lax
from jax.experimental import pallas as pl
from jax.experimental.pallas import tpu as pltpu
from jax.sharding import PartitionSpec as P

CAP = 8
CORES = 2
LAG = 4
EARLY = 8
PIECES = 4
F32 = jnp.float32
BF16 = jnp.bfloat16
MESH = pl.DeviceIdType.MESH


def nt(a, b):
    return lax.dot_general(a, b, (((1,), (1,)), ((), ())), preferred_element_type=F32)


def nn(a, b):
    return lax.dot_general(a, b, (((1,), (0,)), ((), ())), preferred_element_type=F32)


def tn(a, b):
    return lax.dot_general(a, b, (((0,), (0,)), ((), ())), preferred_element_type=F32)


def kernel(
    sizes,
    ids_hbm, tokens_hbm, cotangent_hbm, gate_hbm, up_hbm, down_hbm,
    out_rows, out_gate, out_up,
    ids, mine, sbuf, afull, wfull, placer, placer_t, acc, gact, tfull, wsum, pbuf, x1, x2, x3, rbuf, back,
    ins, zs, zr, xg_s, xg_r, xh_s, xh_r, ws, wr, vs, vr, bs, br, p1_s, p1_r, p2_s, p2_r, p3_s, p3_r,
    as_s, as_r, ah_s, ah_r, e_s, e_r, f1_s, f1_r, f2_s, f2_r, known, answer,
):
    n_dp, n_expert, n_tensor = sizes
    i, e, t = lax.axis_index("dp"), lax.axis_index("expert"), lax.axis_index("tensor")
    z, core = lax.div(e, CORES), lax.rem(e, CORES)
    chips = n_expert // CORES
    half_ring = chips // 2
    block, features = tokens_hbm.shape
    part = features // n_tensor
    width = part // n_dp
    rows = n_expert * CAP
    hidden = gate_hbm.shape[0]
    half_hidden = hidden // 2
    weights = (gate_hbm, up_hbm, down_hbm)
    i_left, i_opp, i_right = (lax.rem(i + k, n_dp) for k in (n_dp - 1, 2, 1))
    t_left, t_opp, t_right = (lax.rem(t + k, n_tensor) for k in (n_tensor - 1, 2, 1))
    y_peer = ({"dp": i_left}, {"dp": i_right})
    x_peer = ({"tensor": t_left}, {"tensor": t_right})
    TO_LEFT, TO_RIGHT = 0, 1

    def copy(src, dst, send, recv, peer):
        return pltpu.make_async_remote_copy(
            src_ref=src, dst_ref=dst, send_sem=send, recv_sem=recv, device_id=peer, device_id_type=MESH
        )

    barrier = pltpu.get_barrier_semaphore()
    other = z * CORES + 1 - core
    z_next, z_prev = lax.rem(z + 1, chips), lax.rem(z + chips - 1, chips)
    near = y_peer + x_peer + ({"dp": i_opp}, {"tensor": t_opp}, {"expert": other})
    last = z == chips - 1
    ahead, behind = (tuple({"expert": chip * CORES + c} for c in range(CORES)) for chip in (z_next, z_prev))
    z_peer = ({"expert": z_prev * CORES + core}, {"expert": z_next * CORES + core})
    for peer in near + behind:
        pl.semaphore_signal(barrier, inc=1, device_id=peer, device_id_type=MESH)

    @pl.when(z < chips - 1)
    def _():
        for peer in ahead:
            pl.semaphore_signal(barrier, inc=1, device_id=peer, device_id_type=MESH)

    fetch_rows = [pltpu.make_async_copy(ids_hbm, ids, ins.at[0])]
    for kind, array in enumerate((tokens_hbm, cotangent_hbm)):
        for j in range(n_dp):
            columns = pl.ds(pl.multiple_of(j * part + t * width, width), width)
            fetch_rows.append(
                pltpu.make_async_copy(
                    array.at[:, columns], mine.at[kind, :, pl.ds(j * width, width)], ins.at[1 + kind * n_dp + j]
                )
            )
    fetch_weights = [pltpu.make_async_copy(weights[k], wfull.at[k, 3], ins.at[1 + 2 * n_dp + k]) for k in range(3)]
    for fetch in fetch_rows + fetch_weights:
        fetch.start()

    def weight_first(k, d):
        return copy(weights[k], wfull.at[k, 2 if d == TO_LEFT else 0], ws.at[k, d], wr.at[k, d], y_peer[d])

    def weight_second(k, d):
        cut = pl.ds(0 if d == TO_RIGHT else half_hidden, half_hidden)
        return copy(
            wfull.at[k, 0 if d == TO_RIGHT else 2, cut], wfull.at[k, 1, cut], vs.at[k, d], vr.at[k, d], y_peer[d]
        )

    def weight_forward(k):
        for d in range(2):
            weight_first(k, d).wait_recv()
            weight_second(k, d).start()

    @pl.when(z > 0)
    def _():
        pl.semaphore_wait(barrier, len(near) + 2 * CORES)

    @pl.when(z == 0)
    def _():
        pl.semaphore_wait(barrier, len(near) + CORES)

    @pl.when(last)
    def _():
        for peer in ahead:
            pl.semaphore_signal(answer.at[0], inc=1, device_id=peer, device_id_type=MESH)

    for k in range(3):
        for d in range(2):
            weight_first(k, d).start()

    def report(d):
        pl.semaphore_signal(known.at[d], inc=1, device_id=z_peer[d], device_id_type=MESH)

    @pl.when(z == 0)
    def _():
        pl.semaphore_wait(answer.at[0], CORES)

    report(0)
    report(1)

    for fetch in fetch_rows:
        fetch.wait()
    chosen = ids[...]
    onehot = (lax.broadcasted_iota(jnp.int32, (n_expert, block), 0) == chosen).astype(BF16)
    before = (
        lax.broadcasted_iota(jnp.int32, (block, block), 0) < lax.broadcasted_iota(jnp.int32, (block, block), 1)
    ).astype(BF16)
    earlier = nn(onehot, before)
    position = jnp.sum(earlier * onehot.astype(F32), axis=0, keepdims=True).astype(jnp.int32)
    target = chosen * CAP + position
    placer[...] = (lax.broadcasted_iota(jnp.int32, (rows, block), 0) == target).astype(BF16)
    for kind in range(2):
        sbuf[:, pl.ds(kind * part, part)] = nn(placer[...], mine[kind]).astype(BF16)

    def eight(k):
        return pl.ds(pl.multiple_of(k * CAP, CAP), CAP)

    def both(k):
        return pl.ds(pl.multiple_of(k * (CORES * CAP), CORES * CAP), CORES * CAP)

    def expert_at(away, c):
        return lax.rem(z + away, chips) * CORES + c

    def dispatch(away, c):
        to = expert_at(away, c)
        return copy(sbuf.at[eight(to)], afull.at[t, eight(e)], zs.at[to], zr.at[e], {"expert": to})

    def arrived(source):
        copy(
            sbuf.at[eight(other)], afull.at[t, eight(source)], zs.at[source], zr.at[source], {"expert": other}
        ).wait_recv()

    def send_to(away):
        for c in range(CORES):
            dispatch(away, c).start()

    dispatch(0, 1 - core).start()
    own = pltpu.make_async_copy(sbuf.at[eight(e)], afull.at[t, eight(e)], zs.at[e])
    own.start()
    send_to(1)
    send_to(chips - 1)

    def send_further(m, carry):
        for d in range(2):
            pl.semaphore_wait(known.at[d], 1)
            report(d)
        send_to(m + 1)
        send_to(chips - m - 1)
        return carry

    lax.fori_loop(1, half_ring - 1, send_further, 0)
    for d in range(2):
        pl.semaphore_wait(known.at[d], 1)
    send_to(half_ring)

    def chunk(m):
        odd = lax.rem(m, 2)
        return lax.rem(z + odd * (chips - lax.div(m + 1, 2)) + (1 - odd) * lax.div(m, 2), chips)

    def spread_first(q, m, d):
        c = both(chunk(m))
        return copy(afull.at[q, c], afull.at[q, c], xg_s.at[d, m], xg_r.at[d, m], x_peer[d])

    def spread_second(q, m, d):
        c = eight(chunk(m) * CORES + (0 if d == TO_RIGHT else 1))
        return copy(afull.at[q, c], afull.at[q, c], xh_s.at[d, m], xh_r.at[d, m], x_peer[d])

    def spread_own(m):
        for d in range(2):
            spread_first(t, m, d).start()

    def forward(m):
        for d in range(2):
            from_q = t_left if d == TO_RIGHT else t_right
            spread_first(from_q, m, d).wait_recv()
            spread_second(from_q, m, d).start()

    def take(m, carry):
        for c in range(CORES):
            arrived(chunk(m) * CORES + c)
        spread_own(m)
        return carry

    def take_and_forward(m, carry):
        take(m, carry)
        forward(m - LAG)
        return carry

    def forward_only(m, carry):
        forward(m)
        return carry

    def exchange(r):
        j = lax.rem(i + r, n_dp)
        columns = pl.ds(pl.multiple_of(j * width, width), width)
        return copy(afull.at[t, :, columns], tfull.at[t, r - 1], e_s.at[r - 1], e_r.at[r - 1], {"dp": j})

    def share_first(d):
        return copy(tfull.at[t], tfull.at[t], f1_s.at[d], f1_r.at[d], x_peer[d])

    def share_second(q, d):
        cut = pl.ds(0 if d == TO_RIGHT else rows // 2, rows // 2)
        return copy(tfull.at[q, :, cut], tfull.at[q, :, cut], f2_s.at[d], f2_r.at[d], x_peer[d])

    def exchange_start():
        for r in range(1, n_dp):
            exchange(r).start()

    def share_start():
        for r in range(1, n_dp):
            exchange(r).wait_recv()
        for d in range(2):
            share_first(d).start()

    def share_forward():
        for d in range(2):
            share_first(d).wait_recv()
            share_second(t_left if d == TO_RIGHT else t_right, d).start()

    early = z < 3 * chips // EARLY
    late = z >= 3 * chips // EARLY

    own.wait()
    arrived(other)
    spread_own(0)
    lax.fori_loop(1, LAG, take, 0)
    lax.fori_loop(LAG, 11, take_and_forward, 0)
    weight_forward(0)
    lax.fori_loop(11, 15, take_and_forward, 0)
    weight_forward(1)
    lax.fori_loop(15, chips, take_and_forward, 0)
    pl.when(early)(exchange_start)
    lax.fori_loop(chips - LAG, chips, forward_only, 0)
    weight_forward(2)
    pl.when(late)(exchange_start)

    def finish_rows(m, carry):
        for d in range(2):
            spread_second(t_opp, m, d).wait_recv()
        return carry

    lax.fori_loop(0, chips, finish_rows, 0)
    pl.when(early)(share_start)
    for fetch in fetch_weights:
        fetch.wait()

    def rows_of(j, kind):
        columns = pl.ds(pl.multiple_of(kind * part + j * width, width), width)
        return jnp.concatenate([afull[q, :, columns] for q in range(n_tensor)], axis=1)

    def product(k, kind):
        acc[k] = nt(wfull[k, 3], rows_of(i, kind))
        acc[k] += nt(wfull[k, 0], rows_of(i_left, kind))
        acc[k] += nt(wfull[k, 2], rows_of(i_right, kind))

    def product_end(k, kind):
        for d in range(2):
            weight_second(k, d).wait_recv()
        return acc[k] + nt(wfull[k, 1], rows_of(i_opp, kind))

    for k, kind in enumerate((0, 0, 1)):
        product(k, kind)
    gate_act = product_end(0, 0)
    sigmoid_gate = jax.nn.sigmoid(gate_act)
    acc[0] = gate_act * sigmoid_gate
    acc[1] = product_end(1, 0) * (sigmoid_gate * (1.0 + gate_act * (1.0 - sigmoid_gate)))
    hidden_grad = product_end(2, 1)
    gact[3, 0] = (hidden_grad * acc[1]).astype(BF16)
    gact[3, 1] = (hidden_grad * acc[0]).astype(BF16)

    def act_first(k, d):
        return copy(gact.at[3, k], gact.at[2 if d == TO_LEFT else 0, k], as_s.at[k, d], as_r.at[k, d], y_peer[d])

    def act_second(k, d):
        cut = pl.ds(0 if d == TO_RIGHT else half_hidden, half_hidden)
        return copy(
            gact.at[0 if d == TO_RIGHT else 2, k, cut], gact.at[1, k, cut], ah_s.at[k, d], ah_r.at[k, d], y_peer[d]
        )

    def act_forward(k):
        for d in range(2):
            act_first(k, d).wait_recv()
            act_second(k, d).start()

    for k in range(2):
        for d in range(2):
            act_first(k, d).start()

    def input_term(r):
        q = lax.rem(t + r, n_tensor)
        slot = 3 - lax.rem(q + n_dp - i, n_dp)
        pbuf[r] = (tn(gact[3, 0], wfull[0, slot]) + tn(gact[3, 1], wfull[1, slot])).astype(BF16)

    size = rows // 2 // PIECES
    cuts = [[pl.ds(h * rows // 2 + p * size, size) for h in range(2)] for p in range(PIECES)]

    def part_hop(d, p):
        cut = cuts[p][0 if d == TO_RIGHT else 1]
        return copy(pbuf.at[2, cut], x1.at[d, p], p1_s.at[d, p], p1_r.at[d, p], x_peer[d])

    def part_last(d, p, h):
        cut = cuts[p][h]
        r = 1 if d == TO_RIGHT else 3
        return copy(pbuf.at[r, cut], x2.at[d, cut], p2_s.at[d, p, h], p2_r.at[d, p, h], x_peer[d])

    def part_far(h):
        return copy(pbuf.at[2, cuts[0][h]], x3.at[h], p3_s.at[h], p3_r.at[h], {"tensor": t_opp})

    def hop(p):
        for d in range(2):
            part_hop(d, p).start()

    def relay(p):
        for d, r, h in ((TO_RIGHT, 1, 0), (TO_LEFT, 3, 1)):
            cut = cuts[p][h]
            part_hop(d, p).wait_recv()
            pbuf[r, cut] = (pbuf[r, cut].astype(F32) + x1[d, p].astype(F32)).astype(BF16)
            part_last(d, p, h).start()

    def own_half(p):
        part_last(TO_RIGHT, p, 1).start()
        part_last(TO_LEFT, p, 0).start()

    def give_back(to):
        return copy(rbuf.at[eight(to)], back.at[eight(e)], bs.at[to], br.at[e], {"expert": to})

    def add_up(p):
        for h in range(2):
            cut = cuts[p][h]
            for d in range(2):
                part_last(d, p, h).wait_recv()
            total = pbuf[0, cut].astype(F32) + x2[0, cut].astype(F32) + x2[1, cut].astype(F32)
            if p == 0:
                part_far(h).wait_recv()
                total += x3[h].astype(F32)
            rbuf[cut, :] = total.astype(BF16)

    def give(place):
        for h in range(2):
            to = h * (n_expert // 2) + place

            @pl.when(to != e)
            def _():
                give_back(to).start()

    def give_piece(p):
        for place in range(p * n_expert // 2 // PIECES, (p + 1) * n_expert // 2 // PIECES):
            give(place)

    input_term(2)
    for h in range(2):
        part_far(h).start()
    hop(1)
    input_term(1)
    input_term(3)
    for h in range(2):
        for d in range(2):
            part_last(d, 0, h).start()
    own_half(1)
    input_term(0)
    hop(2)
    relay(1)
    add_up(0)
    give_piece(0)
    own_half(2)
    hop(3)
    pl.when(early)(share_forward)
    relay(2)
    own_half(3)
    act_forward(0)
    add_up(1)
    give_piece(1)
    relay(3)
    pl.when(late)(share_start)
    add_up(2)
    give_piece(2)
    act_forward(1)
    add_up(3)
    give_piece(3)
    kept = pltpu.make_async_copy(rbuf.at[eight(e)], back.at[eight(e)], bs.at[e])
    kept.start()
    pl.when(late)(share_forward)

    for k in range(2):
        wsum[k] = nn(gact[3, k], rows_of(i, 0))
    for d in range(2):
        share_second(t_opp, d).wait_recv()

    def group_rows(r):
        return jnp.concatenate([tfull[q, r - 1] for q in range(n_tensor)], axis=1)

    for k in range(2):
        wsum[k] += nn(gact[0, k], group_rows(1)) + nn(gact[2, k], group_rows(3))
    for k, out in enumerate((out_gate, out_up)):
        for d in range(2):
            act_second(k, d).wait_recv()
        out[...] = (wsum[k] + nn(gact[1, k], group_rows(2))).astype(BF16)

    def returned(away, c):
        source = expert_at(away, c)
        copy(rbuf.at[eight(other)], back.at[eight(source)], bs.at[other], br.at[source], {"expert": other}).wait_recv()

    def take_back(away, carry):
        for c in range(CORES):
            returned(away, c)
        return carry

    placer_t[...] = placer[...].astype(F32).T.astype(BF16)
    kept.wait()
    returned(0, 1 - core)
    lax.fori_loop(1, chips, take_back, 0)
    out_rows[...] = nn(placer_t[...], back[...]).astype(BF16)

    dispatch(0, 1 - core).wait_send()
    give_back(other).wait_send()

    def sent(away, carry):
        for c in range(CORES):
            dispatch(away, c).wait_send()
            give_back(expert_at(away, c)).wait_send()
        return carry

    lax.fori_loop(1, chips, sent, 0)

    def spread_sent(m, carry):
        for d in range(2):
            spread_first(t, m, d).wait_send()
            spread_second(t_left if d == TO_RIGHT else t_right, m, d).wait_send()
        return carry

    lax.fori_loop(0, chips, spread_sent, 0)
    for r in range(1, n_dp):
        exchange(r).wait_send()
    for d in range(2):
        for k in range(2):
            act_first(k, d).wait_send()
            act_second(k, d).wait_send()
        share_first(d).wait_send()
        share_second(t_left if d == TO_RIGHT else t_right, d).wait_send()
        part_far(d).wait_send()
        for p in range(PIECES):
            if p > 0:
                part_hop(d, p).wait_send()
            for h in range(2):
                part_last(d, p, h).wait_send()
        for k in range(3):
            weight_first(k, d).wait_send()
            weight_second(k, d).wait_send()


def write_out(*refs):
    count = len(refs) // 2
    copies = [pltpu.make_async_copy(refs[n], refs[count + n], refs[-1].at[n]) for n in range(count)]
    for each in copies:
        each.start()
    for each in copies:
        each.wait()


def on_device(sizes, tokens, cotangent, expert_ids, gate_weight, up_weight, down_weight):
    n_dp, n_expert, n_tensor = sizes
    block, features = tokens.shape
    hidden, depth = gate_weight.shape[2], gate_weight.shape[1]
    part, rows, chips = features // n_tensor, n_expert * CAP, n_expert // CORES
    dma = pltpu.SemaphoreType.DMA
    flip = lambda w: jnp.swapaxes(w, 1, 2)[0]
    operands = (expert_ids.reshape(1, block), tokens, cotangent, flip(gate_weight), flip(up_weight), flip(down_weight))
    grad_rows, grad_gate, grad_up = pl.pallas_call(
        functools.partial(kernel, sizes),
        out_shape=(
            jax.ShapeDtypeStruct((block, part), BF16),
            jax.ShapeDtypeStruct((hidden, depth), BF16),
            jax.ShapeDtypeStruct((hidden, depth), BF16),
        ),
        in_specs=[pl.BlockSpec(memory_space=pltpu.HBM)] * 6,
        out_specs=[pl.BlockSpec(memory_space=pltpu.VMEM)] * 3,
        scratch_shapes=[
            pltpu.VMEM((1, block), jnp.int32),
            pltpu.VMEM((2, block, part), BF16),
            pltpu.VMEM((rows, 2 * part), BF16),
            pltpu.VMEM((n_tensor, rows, 2 * part), BF16),
            pltpu.VMEM((3, n_dp, hidden, depth), BF16),
            pltpu.VMEM((rows, block), BF16),
            pltpu.VMEM((block, rows), BF16),
            pltpu.VMEM((3, hidden, rows), F32),
            pltpu.VMEM((n_dp, 2, hidden, rows), BF16),
            pltpu.VMEM((n_tensor, n_dp - 1, rows, part // n_dp), BF16),
            pltpu.VMEM((2, hidden, depth), F32),
            pltpu.VMEM((n_tensor, rows, part), BF16),
            pltpu.VMEM((2, PIECES, rows // 2 // PIECES, part), BF16),
            pltpu.VMEM((2, rows, part), BF16),
            pltpu.VMEM((2, rows // 2 // PIECES, part), BF16),
            pltpu.VMEM((rows, part), BF16),
            pltpu.VMEM((rows, part), BF16),
            dma((1 + 2 * n_dp + 3,)), dma((n_expert,)), dma((n_expert,)),
            dma((2, chips)), dma((2, chips)), dma((2, chips)), dma((2, chips)),
            dma((3, 2)), dma((3, 2)), dma((3, 2)), dma((3, 2)),
            dma((n_expert,)), dma((n_expert,)),
            dma((2, PIECES)), dma((2, PIECES)), dma((2, PIECES, 2)), dma((2, PIECES, 2)), dma((2,)), dma((2,)),
            dma((2, 2)), dma((2, 2)), dma((2, 2)), dma((2, 2)),
            dma((n_dp - 1,)), dma((n_dp - 1,)),
            dma((2,)), dma((2,)), dma((2,)), dma((2,)),
            pltpu.SemaphoreType.REGULAR((2,)),
            pltpu.SemaphoreType.REGULAR((1,)),
        ],
        compiler_params=pltpu.CompilerParams(
            collective_id=0, has_side_effects=True, vmem_limit_bytes=48 << 20
        ),
        name="moe_backward",
    )(*(pltpu.with_memory_space_constraint(a, pltpu.HBM) for a in operands))
    results = (grad_rows, grad_gate, grad_up)
    grad_rows, grad_gate, grad_up = pl.pallas_call(
        write_out,
        out_shape=tuple(jax.ShapeDtypeStruct(r.shape, r.dtype) for r in results),
        in_specs=[pl.BlockSpec(memory_space=pltpu.VMEM)] * 3,
        out_specs=[pl.BlockSpec(memory_space=pltpu.HBM)] * 3,
        scratch_shapes=[dma((3,))],
        compiler_params=pltpu.CompilerParams(vmem_limit_bytes=32 << 20),
        name="write_out",
    )(*results)
    back = lambda g: jnp.swapaxes(g[None], 1, 2)
    return grad_rows, back(grad_gate), back(grad_up)


def solution(mesh):
    sizes = tuple(mesh.shape[a] for a in ("dp", "expert", "tensor"))
    row, weight = P(("dp", "expert"), None), P("expert", "dp", "tensor")
    return jax.shard_map(
        functools.partial(on_device, sizes),
        mesh=mesh,
        in_specs=(row, row, row, weight, weight, weight),
        out_specs=(P(("dp", "expert"), "tensor"), weight, weight),
        check_vma=False,
    )
```

```python
import functools

import jax
import jax.numpy as jnp
from jax import lax
from jax.experimental import pallas as pl
from jax.experimental.pallas import tpu as pltpu
from jax.sharding import PartitionSpec as P

CAP = 8
CORES = 2
LAG = 4

PIECES = 4
F32 = jnp.float32
BF16 = jnp.bfloat16
MESH = pl.DeviceIdType.MESH


def nt(a, b):
    return lax.dot_general(a, b, (((1,), (1,)), ((), ())), preferred_element_type=F32)


def nn(a, b):
    return lax.dot_general(a, b, (((1,), (0,)), ((), ())), preferred_element_type=F32)


def tn(a, b):
    return lax.dot_general(a, b, (((0,), (0,)), ((), ())), preferred_element_type=F32)


def kernel(
    sizes,
    ids_hbm, tokens_hbm, cotangent_hbm, gate_hbm, up_hbm, down_hbm,
    out_rows, out_gate, out_up,
    ids, mine, sbuf, afull, wfull, placer, placer_t, acc, gact, tfull, wsum, pbuf, x1, x2, x3, rbuf, back,
    ins, zs, zr, xg_s, xg_r, xh_s, xh_r, ws, wr, vs, vr, bs, br, p1_s, p1_r, p2_s, p2_r, p3_s, p3_r,
    as_s, as_r, ah_s, ah_r, e_s, e_r, f1_s, f1_r, f2_s, f2_r, known, answer,
):
    n_dp, n_expert, n_tensor = sizes
    i, e, t = lax.axis_index("dp"), lax.axis_index("expert"), lax.axis_index("tensor")
    z, core = lax.div(e, CORES), lax.rem(e, CORES)
    chips = n_expert // CORES
    half_ring = chips // 2
    block, features = tokens_hbm.shape
    part = features // n_tensor
    width = part // n_dp
    rows = n_expert * CAP
    hidden = gate_hbm.shape[0]
    half_hidden = hidden // 2
    weights = (gate_hbm, up_hbm, down_hbm)
    i_left, i_opp, i_right = (lax.rem(i + k, n_dp) for k in (n_dp - 1, 2, 1))
    t_left, t_opp, t_right = (lax.rem(t + k, n_tensor) for k in (n_tensor - 1, 2, 1))
    y_peer = ({"dp": i_left}, {"dp": i_right})
    x_peer = ({"tensor": t_left}, {"tensor": t_right})
    TO_LEFT, TO_RIGHT = 0, 1

    def copy(src, dst, send, recv, peer):
        return pltpu.make_async_remote_copy(
            src_ref=src, dst_ref=dst, send_sem=send, recv_sem=recv, device_id=peer, device_id_type=MESH
        )

    barrier = pltpu.get_barrier_semaphore()
    other = z * CORES + 1 - core
    z_next, z_prev = lax.rem(z + 1, chips), lax.rem(z + chips - 1, chips)
    near = y_peer + x_peer + ({"dp": i_opp}, {"tensor": t_opp}, {"expert": other})
    last = z == chips - 1
    ahead, behind = (tuple({"expert": chip * CORES + c} for c in range(CORES)) for chip in (z_next, z_prev))
    z_peer = ({"expert": z_prev * CORES + core}, {"expert": z_next * CORES + core})
    for peer in near + behind:
        pl.semaphore_signal(barrier, inc=1, device_id=peer, device_id_type=MESH)

    @pl.when(z < chips - 1)
    def _():
        for peer in ahead:
            pl.semaphore_signal(barrier, inc=1, device_id=peer, device_id_type=MESH)

    fetch_rows = [pltpu.make_async_copy(ids_hbm, ids, ins.at[0])]
    for kind, array in enumerate((tokens_hbm, cotangent_hbm)):
        for j in range(n_dp):
            columns = pl.ds(pl.multiple_of(j * part + t * width, width), width)
            fetch_rows.append(
                pltpu.make_async_copy(
                    array.at[:, columns], mine.at[kind, :, pl.ds(j * width, width)], ins.at[1 + kind * n_dp + j]
                )
            )
    fetch_weights = [pltpu.make_async_copy(weights[k], wfull.at[k, 3], ins.at[1 + 2 * n_dp + k]) for k in range(3)]
    for fetch in fetch_rows + fetch_weights:
        fetch.start()

    def weight_first(k, d):
        return copy(weights[k], wfull.at[k, 2 if d == TO_LEFT else 0], ws.at[k, d], wr.at[k, d], y_peer[d])

    def weight_second(k, d):
        cut = pl.ds(0 if d == TO_RIGHT else half_hidden, half_hidden)
        return copy(
            wfull.at[k, 0 if d == TO_RIGHT else 2, cut], wfull.at[k, 1, cut], vs.at[k, d], vr.at[k, d], y_peer[d]
        )

    def weight_forward(k):
        for d in range(2):
            weight_first(k, d).wait_recv()
            weight_second(k, d).start()

    @pl.when(z > 0)
    def _():
        pl.semaphore_wait(barrier, len(near) + 2 * CORES)

    @pl.when(z == 0)
    def _():
        pl.semaphore_wait(barrier, len(near) + CORES)

    @pl.when(last)
    def _():
        for peer in ahead:
            pl.semaphore_signal(answer.at[0], inc=1, device_id=peer, device_id_type=MESH)

    for k in range(3):
        for d in range(2):
            weight_first(k, d).start()

    def report(d):
        pl.semaphore_signal(known.at[d], inc=1, device_id=z_peer[d], device_id_type=MESH)

    @pl.when(z == 0)
    def _():
        pl.semaphore_wait(answer.at[0], CORES)

    report(0)
    report(1)

    for fetch in fetch_rows:
        fetch.wait()
    chosen = ids[...]
    onehot = (lax.broadcasted_iota(jnp.int32, (n_expert, block), 0) == chosen).astype(BF16)
    before = (
        lax.broadcasted_iota(jnp.int32, (block, block), 0) < lax.broadcasted_iota(jnp.int32, (block, block), 1)
    ).astype(BF16)
    earlier = nn(onehot, before)
    position = jnp.sum(earlier * onehot.astype(F32), axis=0, keepdims=True).astype(jnp.int32)
    target = chosen * CAP + position
    placer[...] = (lax.broadcasted_iota(jnp.int32, (rows, block), 0) == target).astype(BF16)
    for kind in range(2):
        sbuf[:, pl.ds(kind * part, part)] = nn(placer[...], mine[kind]).astype(BF16)

    def eight(k):
        return pl.ds(pl.multiple_of(k * CAP, CAP), CAP)

    def both(k):
        return pl.ds(pl.multiple_of(k * (CORES * CAP), CORES * CAP), CORES * CAP)

    def expert_at(away, c):
        return lax.rem(z + away, chips) * CORES + c

    def dispatch(away, c):
        to = expert_at(away, c)
        return copy(sbuf.at[eight(to)], afull.at[t, eight(e)], zs.at[to], zr.at[e], {"expert": to})

    def arrived(source):
        copy(
            sbuf.at[eight(other)], afull.at[t, eight(source)], zs.at[source], zr.at[source], {"expert": other}
        ).wait_recv()

    def send_to(away):
        for c in range(CORES):
            dispatch(away, c).start()

    dispatch(0, 1 - core).start()
    own = pltpu.make_async_copy(sbuf.at[eight(e)], afull.at[t, eight(e)], zs.at[e])
    own.start()
    send_to(1)
    send_to(chips - 1)

    def send_further(m, carry):
        for d in range(2):
            pl.semaphore_wait(known.at[d], 1)
            report(d)
        send_to(m + 1)
        send_to(chips - m - 1)
        return carry

    lax.fori_loop(1, half_ring - 1, send_further, 0)
    for d in range(2):
        pl.semaphore_wait(known.at[d], 1)
    send_to(half_ring)

    def chunk(m):
        odd = lax.rem(m, 2)
        return lax.rem(z + odd * (chips - lax.div(m + 1, 2)) + (1 - odd) * lax.div(m, 2), chips)

    def spread_first(q, m, d):
        c = both(chunk(m))
        return copy(afull.at[q, c], afull.at[q, c], xg_s.at[d, m], xg_r.at[d, m], x_peer[d])

    def spread_second(q, m, d):
        c = eight(chunk(m) * CORES + (0 if d == TO_RIGHT else 1))
        return copy(afull.at[q, c], afull.at[q, c], xh_s.at[d, m], xh_r.at[d, m], x_peer[d])

    def spread_own(m):
        for d in range(2):
            spread_first(t, m, d).start()

    def forward(m):
        for d in range(2):
            from_q = t_left if d == TO_RIGHT else t_right
            spread_first(from_q, m, d).wait_recv()
            spread_second(from_q, m, d).start()

    def take(m, carry):
        for c in range(CORES):
            arrived(chunk(m) * CORES + c)
        spread_own(m)
        return carry

    def take_and_forward(m, carry):
        take(m, carry)
        forward(m - LAG)
        return carry

    def forward_only(m, carry):
        forward(m)
        return carry

    def exchange(r):
        j = lax.rem(i + r, n_dp)
        columns = pl.ds(pl.multiple_of(j * width, width), width)
        return copy(afull.at[t, :, columns], tfull.at[t, r - 1], e_s.at[r - 1], e_r.at[r - 1], {"dp": j})

    def share_first(d):
        return copy(tfull.at[t], tfull.at[t], f1_s.at[d], f1_r.at[d], x_peer[d])

    def share_second(q, d):
        cut = pl.ds(0 if d == TO_RIGHT else rows // 2, rows // 2)
        return copy(tfull.at[q, :, cut], tfull.at[q, :, cut], f2_s.at[d], f2_r.at[d], x_peer[d])

    def exchange_start():
        for r in range(1, n_dp):
            exchange(r).start()

    def share_start():
        for r in range(1, n_dp):
            exchange(r).wait_recv()
        for d in range(2):
            share_first(d).start()

    def share_forward():
        for d in range(2):
            share_first(d).wait_recv()
            share_second(t_left if d == TO_RIGHT else t_right, d).start()

    early = z < chips // 2
    late = z >= chips // 2

    own.wait()
    arrived(other)
    spread_own(0)
    lax.fori_loop(1, LAG, take, 0)
    lax.fori_loop(LAG, 11, take_and_forward, 0)
    weight_forward(0)
    lax.fori_loop(11, 15, take_and_forward, 0)
    weight_forward(1)
    lax.fori_loop(15, chips, take_and_forward, 0)
    pl.when(early)(exchange_start)
    lax.fori_loop(chips - LAG, chips, forward_only, 0)
    weight_forward(2)
    pl.when(late)(exchange_start)

    def finish_rows(m, carry):
        for d in range(2):
            spread_second(t_opp, m, d).wait_recv()
        return carry

    lax.fori_loop(0, chips, finish_rows, 0)
    pl.when(early)(share_start)
    for fetch in fetch_weights:
        fetch.wait()

    def rows_of(j, kind):
        columns = pl.ds(pl.multiple_of(kind * part + j * width, width), width)
        return jnp.concatenate([afull[q, :, columns] for q in range(n_tensor)], axis=1)

    def product(k, kind):
        acc[k] = nt(wfull[k, 3], rows_of(i, kind))
        acc[k] += nt(wfull[k, 0], rows_of(i_left, kind))
        acc[k] += nt(wfull[k, 2], rows_of(i_right, kind))

    def product_end(k, kind):
        for d in range(2):
            weight_second(k, d).wait_recv()
        return acc[k] + nt(wfull[k, 1], rows_of(i_opp, kind))

    for k, kind in enumerate((0, 0, 1)):
        product(k, kind)
    gate_act = product_end(0, 0)
    sigmoid_gate = jax.nn.sigmoid(gate_act)
    acc[0] = gate_act * sigmoid_gate
    acc[1] = product_end(1, 0) * (sigmoid_gate * (1.0 + gate_act * (1.0 - sigmoid_gate)))
    hidden_grad = product_end(2, 1)
    gact[3, 0] = (hidden_grad * acc[1]).astype(BF16)
    gact[3, 1] = (hidden_grad * acc[0]).astype(BF16)

    def act_first(k, d):
        return copy(gact.at[3, k], gact.at[2 if d == TO_LEFT else 0, k], as_s.at[k, d], as_r.at[k, d], y_peer[d])

    def act_second(k, d):
        cut = pl.ds(0 if d == TO_RIGHT else half_hidden, half_hidden)
        return copy(
            gact.at[0 if d == TO_RIGHT else 2, k, cut], gact.at[1, k, cut], ah_s.at[k, d], ah_r.at[k, d], y_peer[d]
        )

    def act_forward(k):
        for d in range(2):
            act_first(k, d).wait_recv()
            act_second(k, d).start()

    for k in range(2):
        for d in range(2):
            act_first(k, d).start()

    def input_term(r):
        q = lax.rem(t + r, n_tensor)
        slot = 3 - lax.rem(q + n_dp - i, n_dp)
        pbuf[r] = (tn(gact[3, 0], wfull[0, slot]) + tn(gact[3, 1], wfull[1, slot])).astype(BF16)

    size = rows // 2 // PIECES
    cuts = [[pl.ds(h * rows // 2 + p * size, size) for h in range(2)] for p in range(PIECES)]

    def part_hop(d, p):
        cut = cuts[p][0 if d == TO_RIGHT else 1]
        return copy(pbuf.at[2, cut], x1.at[d, p], p1_s.at[d, p], p1_r.at[d, p], x_peer[d])

    def part_last(d, p, h):
        cut = cuts[p][h]
        r = 1 if d == TO_RIGHT else 3
        return copy(pbuf.at[r, cut], x2.at[d, cut], p2_s.at[d, p, h], p2_r.at[d, p, h], x_peer[d])

    def part_far(h):
        return copy(pbuf.at[2, cuts[0][h]], x3.at[h], p3_s.at[h], p3_r.at[h], {"tensor": t_opp})

    def hop(p):
        for d in range(2):
            part_hop(d, p).start()

    def relay(p):
        for d, r, h in ((TO_RIGHT, 1, 0), (TO_LEFT, 3, 1)):
            cut = cuts[p][h]
            part_hop(d, p).wait_recv()
            pbuf[r, cut] = (pbuf[r, cut].astype(F32) + x1[d, p].astype(F32)).astype(BF16)
            part_last(d, p, h).start()

    def own_half(p):
        part_last(TO_RIGHT, p, 1).start()
        part_last(TO_LEFT, p, 0).start()

    def give_back(to):
        return copy(rbuf.at[eight(to)], back.at[eight(e)], bs.at[to], br.at[e], {"expert": to})

    def add_up(p):
        for h in range(2):
            cut = cuts[p][h]
            for d in range(2):
                part_last(d, p, h).wait_recv()
            total = pbuf[0, cut].astype(F32) + x2[0, cut].astype(F32) + x2[1, cut].astype(F32)
            if p == 0:
                part_far(h).wait_recv()
                total += x3[h].astype(F32)
            rbuf[cut, :] = total.astype(BF16)

    def give(place):
        for h in range(2):
            to = h * (n_expert // 2) + place

            @pl.when(to != e)
            def _():
                give_back(to).start()

    def give_piece(p):
        for place in range(p * n_expert // 2 // PIECES, (p + 1) * n_expert // 2 // PIECES):
            give(place)

    input_term(2)
    for h in range(2):
        part_far(h).start()
    hop(1)
    input_term(1)
    input_term(3)
    for h in range(2):
        for d in range(2):
            part_last(d, 0, h).start()
    own_half(1)
    input_term(0)
    hop(2)
    relay(1)
    add_up(0)
    give_piece(0)
    own_half(2)
    hop(3)
    pl.when(early)(share_forward)
    relay(2)
    own_half(3)
    act_forward(0)
    add_up(1)
    give_piece(1)
    relay(3)
    pl.when(late)(share_start)
    add_up(2)
    give_piece(2)
    act_forward(1)
    add_up(3)
    give_piece(3)
    kept = pltpu.make_async_copy(rbuf.at[eight(e)], back.at[eight(e)], bs.at[e])
    kept.start()
    pl.when(late)(share_forward)

    for k in range(2):
        wsum[k] = nn(gact[3, k], rows_of(i, 0))
    for d in range(2):
        share_second(t_opp, d).wait_recv()

    def group_rows(r):
        return jnp.concatenate([tfull[q, r - 1] for q in range(n_tensor)], axis=1)

    for k in range(2):
        wsum[k] += nn(gact[0, k], group_rows(1)) + nn(gact[2, k], group_rows(3))
    for k, out in enumerate((out_gate, out_up)):
        for d in range(2):
            act_second(k, d).wait_recv()
        out[...] = (wsum[k] + nn(gact[1, k], group_rows(2))).astype(BF16)

    def returned(away, c):
        source = expert_at(away, c)
        copy(rbuf.at[eight(other)], back.at[eight(source)], bs.at[other], br.at[source], {"expert": other}).wait_recv()

    def take_back(away, carry):
        for c in range(CORES):
            returned(away, c)
        return carry

    placer_t[...] = placer[...].astype(F32).T.astype(BF16)
    kept.wait()
    returned(0, 1 - core)
    lax.fori_loop(1, chips, take_back, 0)
    out_rows[...] = nn(placer_t[...], back[...]).astype(BF16)

    dispatch(0, 1 - core).wait_send()
    give_back(other).wait_send()

    def sent(away, carry):
        for c in range(CORES):
            dispatch(away, c).wait_send()
            give_back(expert_at(away, c)).wait_send()
        return carry

    lax.fori_loop(1, chips, sent, 0)

    def spread_sent(m, carry):
        for d in range(2):
            spread_first(t, m, d).wait_send()
            spread_second(t_left if d == TO_RIGHT else t_right, m, d).wait_send()
        return carry

    lax.fori_loop(0, chips, spread_sent, 0)
    for r in range(1, n_dp):
        exchange(r).wait_send()
    for d in range(2):
        for k in range(2):
            act_first(k, d).wait_send()
            act_second(k, d).wait_send()
        share_first(d).wait_send()
        share_second(t_left if d == TO_RIGHT else t_right, d).wait_send()
        part_far(d).wait_send()
        for p in range(PIECES):
            if p > 0:
                part_hop(d, p).wait_send()
            for h in range(2):
                part_last(d, p, h).wait_send()
        for k in range(3):
            weight_first(k, d).wait_send()
            weight_second(k, d).wait_send()


def write_out(*refs):
    count = len(refs) // 2
    copies = [pltpu.make_async_copy(refs[n], refs[count + n], refs[-1].at[n]) for n in range(count)]
    for each in copies:
        each.start()
    for each in copies:
        each.wait()


def on_device(sizes, tokens, cotangent, expert_ids, gate_weight, up_weight, down_weight):
    n_dp, n_expert, n_tensor = sizes
    block, features = tokens.shape
    hidden, depth = gate_weight.shape[2], gate_weight.shape[1]
    part, rows, chips = features // n_tensor, n_expert * CAP, n_expert // CORES
    dma = pltpu.SemaphoreType.DMA
    flip = lambda w: jnp.swapaxes(w, 1, 2)[0]
    operands = (expert_ids.reshape(1, block), tokens, cotangent, flip(gate_weight), flip(up_weight), flip(down_weight))
    grad_rows, grad_gate, grad_up = pl.pallas_call(
        functools.partial(kernel, sizes),
        out_shape=(
            jax.ShapeDtypeStruct((block, part), BF16),
            jax.ShapeDtypeStruct((hidden, depth), BF16),
            jax.ShapeDtypeStruct((hidden, depth), BF16),
        ),
        in_specs=[pl.BlockSpec(memory_space=pltpu.HBM)] * 6,
        out_specs=[pl.BlockSpec(memory_space=pltpu.VMEM)] * 3,
        scratch_shapes=[
            pltpu.VMEM((1, block), jnp.int32),
            pltpu.VMEM((2, block, part), BF16),
            pltpu.VMEM((rows, 2 * part), BF16),
            pltpu.VMEM((n_tensor, rows, 2 * part), BF16),
            pltpu.VMEM((3, n_dp, hidden, depth), BF16),
            pltpu.VMEM((rows, block), BF16),
            pltpu.VMEM((block, rows), BF16),
            pltpu.VMEM((3, hidden, rows), F32),
            pltpu.VMEM((n_dp, 2, hidden, rows), BF16),
            pltpu.VMEM((n_tensor, n_dp - 1, rows, part // n_dp), BF16),
            pltpu.VMEM((2, hidden, depth), F32),
            pltpu.VMEM((n_tensor, rows, part), BF16),
            pltpu.VMEM((2, PIECES, rows // 2 // PIECES, part), BF16),
            pltpu.VMEM((2, rows, part), BF16),
            pltpu.VMEM((2, rows // 2 // PIECES, part), BF16),
            pltpu.VMEM((rows, part), BF16),
            pltpu.VMEM((rows, part), BF16),
            dma((1 + 2 * n_dp + 3,)), dma((n_expert,)), dma((n_expert,)),
            dma((2, chips)), dma((2, chips)), dma((2, chips)), dma((2, chips)),
            dma((3, 2)), dma((3, 2)), dma((3, 2)), dma((3, 2)),
            dma((n_expert,)), dma((n_expert,)),
            dma((2, PIECES)), dma((2, PIECES)), dma((2, PIECES, 2)), dma((2, PIECES, 2)), dma((2,)), dma((2,)),
            dma((2, 2)), dma((2, 2)), dma((2, 2)), dma((2, 2)),
            dma((n_dp - 1,)), dma((n_dp - 1,)),
            dma((2,)), dma((2,)), dma((2,)), dma((2,)),
            pltpu.SemaphoreType.REGULAR((2,)),
            pltpu.SemaphoreType.REGULAR((1,)),
        ],
        compiler_params=pltpu.CompilerParams(
            collective_id=0, has_side_effects=True, vmem_limit_bytes=48 << 20
        ),
        name="moe_backward",
    )(*(pltpu.with_memory_space_constraint(a, pltpu.HBM) for a in operands))
    results = (grad_rows, grad_gate, grad_up)
    grad_rows, grad_gate, grad_up = pl.pallas_call(
        write_out,
        out_shape=tuple(jax.ShapeDtypeStruct(r.shape, r.dtype) for r in results),
        in_specs=[pl.BlockSpec(memory_space=pltpu.VMEM)] * 3,
        out_specs=[pl.BlockSpec(memory_space=pltpu.HBM)] * 3,
        scratch_shapes=[dma((3,))],
        compiler_params=pltpu.CompilerParams(vmem_limit_bytes=32 << 20),
        name="write_out",
    )(*results)
    back = lambda g: jnp.swapaxes(g[None], 1, 2)
    return grad_rows, back(grad_gate), back(grad_up)


def solution(mesh):
    sizes = tuple(mesh.shape[a] for a in ("dp", "expert", "tensor"))
    row, weight = P(("dp", "expert"), None), P("expert", "dp", "tensor")
    return jax.shard_map(
        functools.partial(on_device, sizes),
        mesh=mesh,
        in_specs=(row, row, row, weight, weight, weight),
        out_specs=(P(("dp", "expert"), "tensor"), weight, weight),
        check_vma=False,
    )
```
